512 devices in a mesh: row: 32 (over z_lo, y), col: 16 (over z_hi, x, core).
Axes of the slice: x: 4, y: 4, z: 16 (z_hi: 2, z_lo: 8; z = z_hi * 8 + z_lo), core: 2. Of those that a mesh axis runs over, the one named last changes fastest.
Arguments:
- tile_values: bfloat16 [32, 16, 4, 256, 256], P('row', 'col'), may hold values from -0.125 to 0.125
- tile_row: int32 [32, 16, 4], P('row', 'col'), may hold values from 0 to 15
- tile_col: int32 [32, 16, 4], P('row', 'col'), may hold values from 0 to 31
- basis_init: bfloat16 [32, 131072], P(None, ('col', 'row')), may hold values from -6 to 6
Outputs:
- ritz_basis: float32 [32, 131072], P(None, ('col', 'row'))
- residual: float32 [32, 131072], P(None, ('col', 'row'))
- projected: float32 [32, 32], replicated
The draws below stay inside these ranges and needn't reach their ends.
Inputs may be any that keep to these rules, and one draw needn't show every extreme that they name: `tile_row`: coordinates may repeat within a pair of blocks; repeated tiles add. `tile_col`: coordinates may repeat within a pair of blocks; repeated tiles add.
All inputs are finite; a program needn't handle non-finite values.
Results may differ from the reference program's by a relative error of at most 0.013.
Values may be sent and summed in bfloat16 or wider, within the bound.
No kernel may reach another device: no remote copies, remote signals or barrier semaphores. Data moves between devices by JAX's collectives and lax.ppermute only.
A program may use at most 64 MiB of HBM per device.

```python
import jax
import jax.numpy as jnp
from jax import lax

K = 32
TB = 256
TILES = 4
M = 256
ITERS = 1
N = 131072
N_ROW = 32
N_COL = 16


def plant(values, own_key, low, largest):
    longest = values.shape.index(max(values.shape))
    spots = []
    for shift in (0, 1):
        where = [jax.random.randint(jax.random.fold_in(own_key, axis), (), 0, length) for axis, length in enumerate(values.shape)]
        where[longest] = (where[longest] + shift) % values.shape[longest]
        spots.append(tuple(where))
    return values.at[spots[0]].set(low).at[spots[1]].set(largest)


def level_of(key, shape, split, low, top_value):
    factor_of = 1.0
    for dim, parts in split:
        heights = jax.random.uniform(jax.random.fold_in(jax.random.fold_in(key, 6), dim), (parts,), jnp.float32, low / len(split), top_value / len(split))
        factor_of = factor_of * jnp.repeat(jnp.exp(heights), shape[dim] // parts).reshape((-1,) + (1,) * (len(shape) - 1 - dim))
    return factor_of


def bell_draw(key, shape, width, reach, split=(), kind=jnp.bfloat16):
    drawn = width * jax.random.normal(key, shape, jnp.float32)
    if split:
        drawn = drawn * level_of(key, shape, split, -0.22, 0.18)
    return jnp.clip(drawn, -reach, reach).astype(kind)


def setup_inputs(seed: int = 0) -> dict:
    keys = jax.random.split(jax.random.key(seed), 5)
    tile_values = bell_draw(keys[0], (N_ROW, N_COL, TILES, TB, TB), (2 * TILES * TB * TB // M) ** -0.5, 0.125, ((0, 32), (1, 16)))
    tile_row = plant(jax.random.randint(keys[1], (N_ROW, N_COL, TILES), 0, N_COL * M // TB), jax.random.fold_in(keys[1], 1), 0, (N_COL * M // TB) - 1).astype(jnp.int32)
    tile_col = plant(jax.random.randint(keys[2], (N_ROW, N_COL, TILES), 0, N_ROW * M // TB), jax.random.fold_in(keys[2], 1), 0, (N_ROW * M // TB) - 1).astype(jnp.int32)
    basis_init = bell_draw(keys[3], (K, N), 1.0, 6.0, ((1, 512),))
    return dict(tile_values=tile_values, tile_row=tile_row, tile_col=tile_col, basis_init=basis_init)


def exact_dot(left, right):
    return jnp.dot(left, right, precision=lax.Precision.HIGHEST)

def bucket(contrib, index, slots):
    tile_size = contrib.shape[-1]
    onehot_table = (index[:, None] == jnp.arange(slots, dtype=jnp.int32)[None, :]).astype(contrib.dtype)
    summed = jnp.einsum('ktb,tn->knb', contrib, onehot_table, precision=lax.Precision.HIGHEST)
    return summed.reshape(contrib.shape[0], slots * tile_size)

def partials(tile_block, tile_rows, tile_cols, column_block, row_block):
    tile_size = tile_block.shape[-1]
    vector_count = column_block.shape[0]
    col_tiles = column_block.shape[1] // tile_size
    row_tiles = row_block.shape[1] // tile_size
    weights = tile_block.astype(jnp.float32)
    picked = column_block.reshape(vector_count, col_tiles, tile_size)[:, tile_cols].astype(jnp.float32)
    direct = jnp.einsum('ktj,tij->kti', picked, weights, precision=lax.Precision.HIGHEST)
    mirror_pick = row_block.reshape(vector_count, row_tiles, tile_size)[:, tile_rows].astype(jnp.float32)
    mirror = jnp.einsum('kti,tij->ktj', mirror_pick, weights, precision=lax.Precision.HIGHEST)
    direct_part = lax.optimization_barrier(bucket(direct, tile_rows, row_tiles).astype(jnp.bfloat16)).astype(jnp.float32)
    mirror_part = lax.optimization_barrier(bucket(mirror, tile_cols, col_tiles).astype(jnp.bfloat16)).astype(jnp.float32)
    return (direct_part, mirror_part)

def apply_hamiltonian(tile_values, tile_row, tile_col, vectors_bf):
    vector_count = vectors_bf.shape[0]
    blocked = vectors_bf.reshape(vector_count, N_COL, N_ROW, M)
    column_blocks = jnp.transpose(blocked, (1, 0, 2, 3)).reshape(N_COL, vector_count, N_ROW * M)

    def one_row(running, row_index):
        row_block = lax.dynamic_index_in_dim(blocked, row_index, 2, keepdims=False).reshape(vector_count, N_COL * M)
        tiles_here = lax.dynamic_index_in_dim(tile_values, row_index, 0, keepdims=False)
        rows_here = lax.dynamic_index_in_dim(tile_row, row_index, 0, keepdims=False)
        cols_here = lax.dynamic_index_in_dim(tile_col, row_index, 0, keepdims=False)
        direct_parts, mirror_parts = jax.vmap(partials, in_axes=(0, 0, 0, 0, None))(tiles_here, rows_here, cols_here, column_blocks, row_block)
        return (running + mirror_parts, jnp.sum(direct_parts, axis=0))
    mirror_sum, direct_rows = lax.scan(one_row, jnp.zeros((N_COL, vector_count, N_ROW * M), jnp.float32), jnp.arange(N_ROW, dtype=jnp.int32))
    direct_full = jnp.transpose(direct_rows.reshape(N_ROW, vector_count, N_COL, M), (1, 2, 0, 3))
    mirror_full = jnp.transpose(mirror_sum.reshape(N_COL, vector_count, N_ROW, M), (1, 0, 2, 3))
    return (direct_full + mirror_full).reshape(vector_count, N_COL * N_ROW * M)

def reference(tile_values, tile_row, tile_col, basis_init):
    total_rows = N_ROW * N_COL * M
    current = basis_init
    ritz_basis = basis_init.astype(jnp.float32)
    for iteration in range(ITERS):
        product_block = apply_hamiltonian(tile_values, tile_row, tile_col, current)
        gram_matrix = exact_dot(product_block, product_block.T) / total_rows
        factor = jnp.linalg.cholesky(gram_matrix)
        ritz_basis = lax.linalg.triangular_solve(factor, product_block, left_side=True, lower=True)
        current = ritz_basis.astype(jnp.bfloat16)
    product_block = apply_hamiltonian(tile_values, tile_row, tile_col, current)
    projected = exact_dot(ritz_basis, product_block.T) / total_rows
    residual = product_block - exact_dot(projected.T, ritz_basis)
    return (ritz_basis, residual, projected)
```

```python
import functools

import jax
import jax.numpy as jnp
from jax import lax
from jax.experimental import pallas as pl
from jax.experimental.pallas import tpu as pltpu
from jax.sharding import Mesh
from jax.sharding import PartitionSpec as P

Z_HI, X_CORE = ("col_0", ("col_1", "col_2"))
Z_LO, Y = ("row_0", "row_1")
COL = ("col_0", "col_1", "col_2")
ROW = ("row_0", "row_1")
COL_ROW = ("col_0", "col_1", "col_2", "row_0", "row_1")
HIGHEST = lax.Precision.HIGHEST
INTERPRET = False


def exchange(parts, axis):
    return lax.all_to_all(parts, axis, 0, 0, tiled=True)


def spread(value, axis):
    length = lax.axis_size(axis)
    return exchange(jnp.broadcast_to(value[None], (length, *value.shape)), axis)


def partner(value):
    return lax.ppermute(value, Z_HI, [(0, 1), (1, 0)])


def split_bits(small, width):
    pieces = []
    rest = small
    for _ in range(3):
        piece = lax.reduce_precision(rest, 8, 7)
        pieces.append(piece)
        rest = rest - piece
    joined = jnp.concatenate(pieces, axis=-1).astype(jnp.bfloat16)
    return jnp.pad(joined, [(0, 0), (0, width - joined.shape[-1])])


def summed_bits(blocks):
    count = blocks.shape[-2]
    wide = blocks[..., : 3 * count].astype(jnp.float32)
    total = (wide[..., 2 * count :] + wide[..., count : 2 * count]) + wide[..., :count]
    return total.sum(axis=0)


def tile_kernel(
    pair_ref, column_ref, row_ref, tile_ref, direct_ref, mirror_ref, form_ref, sums_ref,
    *, tiles, y_count, xc_count,
):
    side = pair_ref[2 * tiles]
    direct_slots, mirror_slots = ([], [])
    form = jnp.zeros(form_ref.shape, jnp.float32)
    for t in range(tiles):
        i = pair_ref[t]
        j = pair_ref[tiles + t]
        from_column = column_ref[lax.rem(j, y_count), lax.div(j, y_count)]
        half = lax.rem(lax.div(i, xc_count) + side, 2)
        from_row = row_ref[lax.rem(i, xc_count), half]
        direct = lax.dot_general(
            from_column, tile_ref[t], (((1,), (1,)), ((), ())), preferred_element_type=jnp.float32
        )
        sums_ref[t] = direct
        sums_ref[tiles + t] = jnp.dot(from_row, tile_ref[t], preferred_element_type=jnp.float32)
        form += lax.dot_general(
            from_row.astype(jnp.float32), direct, (((1,), (1,)), ((), ())),
            precision=HIGHEST, preferred_element_type=jnp.float32,
        )
        direct_slots.append((i, lax.rem(i, xc_count), half))
        mirror_slots.append((j, lax.rem(j, y_count), lax.div(j, y_count)))
    form_ref[...] = form
    direct_ref[...] = jnp.zeros_like(direct_ref)
    mirror_ref[...] = jnp.zeros_like(mirror_ref)
    for base, slots, out_ref in ((0, direct_slots, direct_ref), (tiles, mirror_slots, mirror_ref)):
        for t in range(tiles):
            total = sums_ref[base + t]
            for other in range(tiles):
                if other != t:
                    same = (slots[other][0] == slots[t][0]).astype(jnp.float32)
                    total = total + same * sums_ref[base + other]
            out_ref[slots[t][1], slots[t][2]] = total.astype(jnp.bfloat16)


def tile_products(pairs, column_block, row_block, tiles):
    vectors, size = column_block.shape[-2:]
    vmem = pl.BlockSpec(memory_space=pltpu.VMEM)
    z_count = lax.axis_size(Z_LO)
    return pl.pallas_call(
        functools.partial(
            tile_kernel,
            tiles=tiles.shape[0],
            y_count=column_block.shape[0],
            xc_count=row_block.shape[0],
        ),
        out_shape=(
            jax.ShapeDtypeStruct((row_block.shape[0], 2, vectors, size), jnp.bfloat16),
            jax.ShapeDtypeStruct((column_block.shape[0], z_count, vectors, size), jnp.bfloat16),
            jax.ShapeDtypeStruct((vectors, vectors), jnp.float32),
        ),
        in_specs=[pl.BlockSpec(memory_space=pltpu.SMEM), vmem, vmem, vmem],
        out_specs=(vmem, vmem, vmem),
        scratch_shapes=[pltpu.VMEM((2 * tiles.shape[0], vectors, size), jnp.float32)],
        interpret=INTERPRET,
        name="tile_products",
    )(pairs, column_block, row_block, tiles)


def shards(tile_values, tile_row, tile_col, basis_init):
    tiles = tile_values[0, 0]
    side = lax.axis_index(Z_HI).astype(jnp.int32)
    pairs = jnp.concatenate([tile_row[0, 0], tile_col[0, 0], side[None]])
    vectors, size = basis_init.shape
    total_rows = size * lax.axis_size(COL_ROW)
    f32 = jnp.float32

    other = partner(basis_init)
    column_block = spread(spread(basis_init, Z_LO), Y)
    row_block = spread(jnp.stack([basis_init, other]), X_CORE)
    direct, mirror, _ = tile_products(pairs, column_block, row_block, tiles)
    direct = exchange(direct, X_CORE).astype(f32).sum(axis=0)
    far = partner(direct[1].astype(jnp.bfloat16))
    mirror = exchange(mirror, Y).astype(f32).sum(axis=0)
    mirror = exchange(mirror.astype(jnp.bfloat16), Z_LO).astype(f32).sum(axis=0)
    image = direct[0] + far.astype(f32) + mirror

    gram = jnp.dot(image, image.T, precision=HIGHEST)
    current = image.astype(jnp.bfloat16)
    other = partner(current)
    by_z = spread(jnp.stack([current, split_bits(gram, size)]), Z_LO)
    gram = summed_bits(by_z[:, 1])
    by_y = spread(jnp.concatenate([by_z[:, 0], split_bits(gram, size)[None]]), Y)
    gram = summed_bits(by_y[:, -1])
    by_xc = spread(jnp.stack([current, other, split_bits(gram, size)]), X_CORE)
    gram = summed_bits(by_xc[:, -1])
    direct, mirror, form = tile_products(pairs, by_y, by_xc, tiles)
    count = direct.shape[0]
    form_block = jnp.broadcast_to(split_bits(form, size)[None, None], (count, 1, vectors, size))
    direct = exchange(jnp.concatenate([direct, form_block], axis=1), X_CORE)
    form = summed_bits(direct[:, -1])
    direct = direct[:, :2].astype(f32).sum(axis=0)
    far = partner(jnp.stack([direct[1].astype(jnp.bfloat16), split_bits(gram, size)]))
    gram = gram + summed_bits(far[1:])
    count = mirror.shape[0]
    form_block = jnp.broadcast_to(split_bits(form, size)[None, None], (count, 1, vectors, size))
    mirror = exchange(jnp.concatenate([mirror, form_block], axis=1), Y)
    form = summed_bits(mirror[:, -1])
    mirror = mirror[:, :-1].astype(f32).sum(axis=0).astype(jnp.bfloat16)
    count = mirror.shape[0]
    form_block = jnp.broadcast_to(split_bits(form, size)[None], (count, vectors, size))
    mirror = exchange(jnp.stack([mirror, form_block], axis=1), Z_LO)
    form = summed_bits(mirror[:, 1])
    mirror = mirror[:, 0].astype(f32).sum(axis=0)
    form = form + summed_bits(partner(split_bits(form, size))[None])
    raw_image = direct[0] + far[0].astype(f32) + mirror

    factor = jnp.linalg.cholesky(gram / total_rows)
    inverse = lax.linalg.triangular_solve(
        factor, jnp.eye(vectors, dtype=f32), left_side=True, lower=True
    )
    ritz_basis = jnp.dot(inverse, image, precision=HIGHEST)
    last_image = jnp.dot(inverse, raw_image, precision=HIGHEST)
    form = (form + form.T) / total_rows
    projected = jnp.dot(
        jnp.dot(inverse, form, precision=HIGHEST), inverse.T, precision=HIGHEST
    )
    residual = last_image - jnp.dot(projected.T, ritz_basis, precision=HIGHEST)
    return (ritz_basis, residual, projected)


def solution(mesh):
    finer = Mesh(mesh.devices.reshape(8, 4, 2, 4, 2), ("row_0", "row_1", "col_0", "col_1", "col_2"))
    placed = (P(ROW, COL, None, None, None), P(ROW, COL, None), P(ROW, COL, None), P(None, COL_ROW))
    return jax.shard_map(
        shards,
        mesh=finer,
        in_specs=placed,
        out_specs=(P(None, COL_ROW), P(None, COL_ROW), P()),
        check_vma=False,
    )
```

```python
import functools

import jax
import jax.numpy as jnp
from jax import lax
from jax.experimental import pallas as pl
from jax.experimental.pallas import tpu as pltpu
from jax.sharding import Mesh
from jax.sharding import PartitionSpec as P

Z_HI, X_CORE = ("col_0", ("col_1", "col_2"))
Z_LO, Y = ("row_0", "row_1")
COL = ("col_0", "col_1", "col_2")
ROW = ("row_0", "row_1")
COL_ROW = ("col_0", "col_1", "col_2", "row_0", "row_1")
HIGHEST = lax.Precision.HIGHEST
VMEM = pl.BlockSpec(memory_space=pltpu.VMEM)
SMEM = pl.BlockSpec(memory_space=pltpu.SMEM)
F32, BF16 = (jnp.float32, jnp.bfloat16)
PIECES = 3


def exchange(parts, axis):
    return lax.all_to_all(parts, axis, 0, 0, tiled=True)


def spread(value, axis):
    length = lax.axis_size(axis)
    return exchange(jnp.broadcast_to(value[None], (length, *value.shape)), axis)


def partner(value):
    return lax.ppermute(value, Z_HI, [(0, 1), (1, 0)])


def split_bits(small, width):
    pieces = []
    rest = small
    for _ in range(PIECES):
        piece = lax.reduce_precision(rest, 8, 7)
        pieces.append(piece)
        rest = rest - piece
    joined = jnp.concatenate(pieces, axis=-1).astype(BF16)
    return jnp.pad(joined, [(0, 0), (0, width - joined.shape[-1])])


def summed_bits(blocks):
    count = blocks.shape[-2]
    wide = blocks[..., : PIECES * count].astype(F32)
    total = (wide[..., 2 * count :] + wide[..., count : 2 * count]) + wide[..., :count]
    return total.sum(axis=0)


def store_bits(out_ref, place, small):
    count = small.shape[-1]
    out_ref[place] = jnp.zeros(out_ref.shape[len(place) :], out_ref.dtype)
    rest = small
    for k in range(PIECES):
        piece = rest.astype(BF16)
        out_ref[(*place, slice(None), pl.ds(k * count, count))] = piece
        rest = rest - piece.astype(F32)


def store_sums(out_ref, slots, sums_ref):
    for t, (index, major, minor) in enumerate(slots):
        total = sums_ref[t]
        for other, (other_index, _, _) in enumerate(slots):
            if other != t:
                total = total + (other_index == index).astype(F32) * sums_ref[other]
        out_ref[major, minor] = total.astype(BF16)


def direct_kernel(pair_ref, column_ref, tile_ref, own_ref, out_ref, sums_ref, *, near, extra):
    tiles = tile_ref.shape[0]
    y_count, xc_count = (column_ref.shape[0], out_ref.shape[0])
    side = pair_ref[2 * tiles]
    for t in range(tiles):
        j = pair_ref[tiles + t]
        from_column = column_ref[lax.rem(j, y_count), lax.div(j, y_count)]
        sums_ref[t] = lax.dot_general(
            from_column, tile_ref[t], (((1,), (1,)), ((), ())), preferred_element_type=F32
        )
    for k in range(xc_count):
        for s in range(near + extra):
            out_ref[k, s] = own_ref[s]
        for s in range(near):
            out_ref[k, near + extra + s] = jnp.zeros(out_ref.shape[2:], BF16)
    slots = []
    for t in range(tiles):
        i = pair_ref[t]
        half = lax.rem(lax.div(i, xc_count) + side, near)
        slots.append((i, lax.rem(i, xc_count), near + extra + half))
    store_sums(out_ref, slots, sums_ref)


def mirror_kernel(
    pair_ref, row_ref, tile_ref, direct_ref, out_ref, own_ref, far_ref, sums_ref, *, near, extra
):
    tiles = tile_ref.shape[0]
    y_count, xc_count = (out_ref.shape[0], row_ref.shape[0])
    side = pair_ref[2 * tiles]
    vectors = own_ref.shape[0]
    form = jnp.zeros((vectors, vectors), F32)
    for t in range(tiles):
        i = pair_ref[t]
        half = lax.rem(lax.div(i, xc_count) + side, near)
        from_row = row_ref[lax.rem(i, xc_count), half]
        sums_ref[t] = jnp.dot(from_row, tile_ref[t], preferred_element_type=F32)
        if extra:
            form += lax.dot_general(
                from_row.astype(F32), direct_ref[t], (((1,), (1,)), ((), ())),
                precision=HIGHEST, preferred_element_type=F32,
            )
    for k in range(y_count):
        for s in range(out_ref.shape[1] - extra):
            out_ref[k, s] = jnp.zeros(out_ref.shape[2:], BF16)
    if extra:
        last = out_ref.shape[1] - 1
        store_bits(out_ref, (0, last), form)
        for k in range(1, y_count):
            out_ref[k, last] = out_ref[0, last]
    slots = []
    for t in range(tiles):
        j = pair_ref[tiles + t]
        slots.append((j, lax.rem(j, y_count), lax.div(j, y_count)))
    store_sums(out_ref, slots, sums_ref)
    for s in range(near):
        total = row_ref[0, near + extra + s].astype(F32)
        for k in range(1, xc_count):
            total = total + row_ref[k, near + extra + s].astype(F32)
        if s == 0:
            own_ref[...] = total
        else:
            far_ref[0] = total.astype(BF16)
    if extra:
        wide = row_ref[0, near].astype(F32)
        for k in range(1, xc_count):
            wide = wide + row_ref[k, near].astype(F32)
        total = (wide[:, 2 * vectors : 3 * vectors] + wide[:, vectors : 2 * vectors]) + wide[:, :vectors]
        store_bits(far_ref, (1,), total)


def product(pairs, tiles, current, gram):
    vectors, size = current.shape
    count = tiles.shape[0]
    near = lax.axis_size(Z_HI)
    y_count, z_count, xc_count = (lax.axis_size(Y), lax.axis_size(Z_LO), lax.axis_size(X_CORE))
    extra = 0 if gram is None else 1
    block = (vectors, size)
    if extra:
        by_z = spread(jnp.stack([current, split_bits(gram, size)]), Z_LO)
        gram = summed_bits(by_z[:, 1])
        by_z = jnp.concatenate([by_z[:, 0], split_bits(gram, size)[None]])
    else:
        by_z = spread(current, Z_LO)
    other = partner(current)
    column_block = spread(by_z, Y)
    own = [current, other]
    if extra:
        gram = summed_bits(column_block[:, -1])
        own.append(split_bits(gram, size))
    send, direct = pl.pallas_call(
        functools.partial(direct_kernel, near=near, extra=extra),
        out_shape=(
            jax.ShapeDtypeStruct((xc_count, 2 * near + extra, *block), BF16),
            jax.ShapeDtypeStruct((count, *block), F32),
        ),
        in_specs=[SMEM, VMEM, VMEM, VMEM],
        out_specs=(VMEM, VMEM),
        name="direct_products",
    )(pairs, column_block, tiles, jnp.stack(own))
    arrived = exchange(send, X_CORE)
    send, own_direct, far = pl.pallas_call(
        functools.partial(mirror_kernel, near=near, extra=extra),
        out_shape=(
            jax.ShapeDtypeStruct((y_count, z_count + extra, *block), BF16),
            jax.ShapeDtypeStruct(block, F32),
            jax.ShapeDtypeStruct((1 + extra, *block), BF16),
        ),
        in_specs=[SMEM, VMEM, VMEM, VMEM],
        out_specs=(VMEM, VMEM, VMEM),
        scratch_shapes=[pltpu.VMEM((count, *block), F32)],
        name="mirror_products",
    )(pairs, arrived, tiles, direct)
    mirror = exchange(send, Y)
    sent, far = (far, partner(far))
    own_sum = mirror[:, :z_count].astype(F32).sum(axis=0).astype(BF16)
    if extra:
        form = split_bits(summed_bits(mirror[:, z_count]), size)
        form_block = jnp.broadcast_to(form[None], (z_count, *block))
        by_z = exchange(jnp.stack([own_sum, form_block], axis=1), Z_LO)
        own_sum = by_z[:, 0].astype(F32).sum(axis=0)
        form = summed_bits(by_z[:, 1])
        gram = summed_bits(jnp.stack([sent[1], far[1]]))
    else:
        own_sum = exchange(own_sum, Z_LO).astype(F32).sum(axis=0)
        form = None
    return own_direct + far[0].astype(F32) + own_sum, gram, form


def steps(tile_values, tile_row, tile_col, basis_init):
    tiles = tile_values[0, 0]
    side = lax.axis_index(Z_HI).astype(jnp.int32)
    pairs = jnp.concatenate([tile_row[0, 0], tile_col[0, 0], side[None]])
    vectors, size = basis_init.shape
    total_rows = size * lax.axis_size(COL_ROW)

    image, _, _ = product(pairs, tiles, basis_init, None)
    gram = jnp.dot(image, image.T, precision=HIGHEST)
    raw_image, gram, form = product(pairs, tiles, image.astype(BF16), gram)
    form = summed_bits(spread(split_bits(form, size)[:, : size // 2], COL))

    factor = jnp.linalg.cholesky(gram / total_rows)
    inverse = lax.linalg.triangular_solve(
        factor, jnp.eye(vectors, dtype=F32), left_side=True, lower=True
    )
    ritz_basis = jnp.dot(inverse, image, precision=HIGHEST)
    last_image = jnp.dot(inverse, raw_image, precision=HIGHEST)
    form = (form + form.T) / total_rows
    projected = jnp.dot(
        jnp.dot(inverse, form, precision=HIGHEST), inverse.T, precision=HIGHEST
    )
    residual = last_image - jnp.dot(projected.T, ritz_basis, precision=HIGHEST)
    return (ritz_basis, residual, projected)


def solution(mesh):
    finer = Mesh(mesh.devices.reshape(8, 4, 2, 4, 2), ("row_0", "row_1", "col_0", "col_1", "col_2"))
    placed = (P(ROW, COL, None, None, None), P(ROW, COL, None), P(ROW, COL, None), P(None, COL_ROW))
    return jax.shard_map(
        steps,
        mesh=finer,
        in_specs=placed,
        out_specs=(P(None, COL_ROW), P(None, COL_ROW), P()),
        check_vma=False,
    )
```

```python
import functools

import jax
import jax.numpy as jnp
from jax import lax
from jax.experimental import pallas as pl
from jax.experimental.pallas import tpu as pltpu
from jax.sharding import Mesh
from jax.sharding import PartitionSpec as P

Z_HI, X_CORE = ("col_0", ("col_1", "col_2"))
Z_LO, Y = ("row_0", "row_1")
Y_X_CORE = ("row_1", "col_1", "col_2")
COL = ("col_0", "col_1", "col_2")
ROW = ("row_0", "row_1")
COL_ROW = ("col_0", "col_1", "col_2", "row_0", "row_1")
HIGHEST = lax.Precision.HIGHEST
VMEM = pl.BlockSpec(memory_space=pltpu.VMEM)
SMEM = pl.BlockSpec(memory_space=pltpu.SMEM)
F32, BF16 = (jnp.float32, jnp.bfloat16)


def placed(value):
    return pltpu.with_memory_space_constraint(value, pltpu.VMEM)


ROWS, LANES, VECTORS = (8, 128, 32)


def exchange(parts, axis):
    return lax.all_to_all(parts, axis, 0, 0, tiled=True)


def call(kernel, *outs, scalars=0, scratch=(), out=pltpu.VMEM):
    def run(*args):
        args = args[:scalars] + tuple(placed(arg) for arg in args[scalars:])
        return pl.pallas_call(
            kernel,
            out_shape=tuple(out(shape, kind) for shape, kind in outs),
            in_specs=[SMEM] * scalars + [VMEM] * (len(args) - scalars),
            out_specs=tuple(VMEM for _ in outs),
            scratch_shapes=list(scratch),
        )(*args)

    return run


def spread(value, axis):
    length = lax.axis_size(axis)
    return exchange(jnp.broadcast_to(value[None], (length, *value.shape)), axis)


def partner(value):
    return lax.ppermute(value, Z_HI, [(0, 1), (1, 0)])


def pack(small):
    return jnp.concatenate([small[k : k + ROWS] for k in range(0, small.shape[0], ROWS)], axis=1)


def unpack(packed):
    return jnp.concatenate([packed[:, k : k + VECTORS] for k in range(0, LANES, VECTORS)], axis=0)


def from_bits(bits):
    wide = bits.astype(F32)
    return wide[..., LANES:] + wide[..., :LANES]


def dot(left, right, left_dim, right_dim):
    return lax.dot_general(
        left, right, (((left_dim,), (right_dim,)), ((), ())),
        precision=HIGHEST, preferred_element_type=F32,
    )


def store_bits(out_ref, place, packed):
    high = packed.astype(BF16)
    out_ref[(*place, slice(0, LANES))] = high
    out_ref[(*place, slice(LANES, 2 * LANES))] = (packed - high.astype(F32)).astype(BF16)


def store_sums(out_ref, slots, sums_ref):
    for t, (index, place) in enumerate(slots):
        total = sums_ref[t]
        for other, (other_index, _) in enumerate(slots):
            if other != t:
                total = total + (other_index == index).astype(F32) * sums_ref[other]
        out_ref[place] = total.astype(BF16)


def span(slot, length, start=0):
    return pl.ds(pl.multiple_of(start + slot * length, length), length)


def direct_kernel(pair_ref, column_ref, tile_ref, own_ref, other_ref, out_ref, sums_ref):
    tiles, vectors = (tile_ref.shape[0], own_ref.shape[0])
    y_count, z_count, xc_count = (*column_ref.shape[:2], out_ref.shape[0])
    side = pair_ref[2 * tiles]
    for t in range(tiles):
        j = pair_ref[tiles + t]
        from_column = column_ref[lax.rem(j, y_count), lax.div(j, y_count), pl.ds(0, vectors)]
        sums_ref[t] = lax.dot_general(
            from_column, tile_ref[t], (((1,), (1,)), ((), ())), preferred_element_type=F32
        )
    blank = jnp.zeros((2 * vectors, out_ref.shape[2]), BF16)
    for k in range(xc_count):
        out_ref[k, pl.ds(0, vectors)] = own_ref[...]
        out_ref[k, pl.ds(vectors, vectors)] = other_ref[...]
        out_ref[k, pl.ds(2 * vectors, 2 * vectors)] = blank
    if out_ref.shape[1] > 4 * vectors:
        total = jnp.zeros((ROWS, LANES), F32)
        for y in range(y_count):
            for z in range(z_count):
                total += from_bits(column_ref[y, z, pl.ds(vectors, ROWS)])
        for k in range(xc_count):
            store_bits(out_ref, (k, pl.ds(4 * vectors, ROWS)), total)
    slots = []
    for t in range(tiles):
        i = pair_ref[t]
        half = lax.rem(lax.div(i, xc_count) + side, 2)
        slots.append((i, (lax.rem(i, xc_count), span(half, vectors, 2 * vectors))))
    store_sums(out_ref, slots, sums_ref)


def mirror_kernel(
    pair_ref, row_ref, tile_ref, direct_ref, out_ref, own_ref, far_ref, sums_ref
):
    tiles, vectors = (tile_ref.shape[0], own_ref.shape[0])
    y_count, xc_count = (out_ref.shape[0], row_ref.shape[0])
    extra = row_ref.shape[1] > 4 * vectors
    side = pair_ref[2 * tiles]
    form = jnp.zeros((vectors, vectors), F32)
    for t in range(tiles):
        i = pair_ref[t]
        half = lax.rem(lax.div(i, xc_count) + side, 2)
        from_row = row_ref[lax.rem(i, xc_count), span(half, vectors)]
        sums_ref[t] = jnp.dot(from_row, tile_ref[t], preferred_element_type=F32)
        if extra:
            form += dot(from_row.astype(F32), direct_ref[t], 1, 1)
    for s in range(2):
        rows = pl.ds((2 + s) * vectors, vectors)
        total = row_ref[0, rows].astype(F32)
        for k in range(1, xc_count):
            total = total + row_ref[k, rows].astype(F32)
        if s == 0:
            own_ref[...] = total
        else:
            far_ref[pl.ds(0, vectors)] = total.astype(BF16)
    if extra:
        total = jnp.zeros((ROWS, LANES), F32)
        for k in range(xc_count):
            total += from_bits(row_ref[k, pl.ds(4 * vectors, ROWS)])
        store_bits(far_ref, (pl.ds(vectors, ROWS),), total)
        store_bits(far_ref, (pl.ds(vectors + ROWS, ROWS),), pack(form))
    for k in range(y_count):
        out_ref[k] = jnp.zeros(out_ref.shape[1:], BF16)
    slots = []
    for t in range(tiles):
        j = pair_ref[tiles + t]
        slots.append((j, (lax.rem(j, y_count), lax.div(j, y_count))))
    store_sums(out_ref, slots, sums_ref)


def image_kernel(direct_ref, far_ref, mirror_ref, image_ref, current_ref, send_ref):
    image = direct_ref[...] + far_ref[...].astype(F32)
    for z in range(mirror_ref.shape[0]):
        image = image + mirror_ref[z].astype(F32)
    image_ref[...] = image
    current = image.astype(BF16)
    current_ref[...] = current
    gram = pack(dot(image, image, 1, 1))
    for z in range(send_ref.shape[0]):
        send_ref[z, pl.ds(0, image.shape[0])] = current
        store_bits(send_ref, (z, pl.ds(image.shape[0], ROWS)), gram)


def middle_kernel(mirror_ref, sent_ref, far_ref, send_ref, gram_ref):
    vectors = gram_ref.shape[0]
    for z in range(send_ref.shape[0]):
        total = mirror_ref[0, z].astype(F32)
        for y in range(1, mirror_ref.shape[0]):
            total = total + mirror_ref[y, z].astype(F32)
        send_ref[z, pl.ds(0, vectors)] = total.astype(BF16)
    rows = pl.ds(vectors, ROWS)
    gram_ref[...] = unpack(from_bits(sent_ref[rows]) + from_bits(far_ref[rows]))
    rows = pl.ds(vectors + ROWS, ROWS)
    form = from_bits(sent_ref[rows]) + from_bits(far_ref[rows])
    for z in range(send_ref.shape[0]):
        store_bits(send_ref, (z, pl.ds(vectors, ROWS)), form)


def last_kernel(direct_ref, far_ref, mirror_ref, image_ref, send_ref):
    vectors = image_ref.shape[0]
    form = jnp.zeros((ROWS, LANES), F32)
    for z in range(mirror_ref.shape[0]):
        form += from_bits(mirror_ref[z, pl.ds(vectors, ROWS)])
    for k in range(send_ref.shape[0]):
        store_bits(send_ref, (k, pl.ds(0, ROWS)), form)
    image = direct_ref[...] + far_ref[pl.ds(0, vectors)].astype(F32)
    for z in range(mirror_ref.shape[0]):
        image = image + mirror_ref[z, pl.ds(0, vectors)].astype(F32)
    image_ref[...] = image


def finish_kernel(bits_ref, inverse_ref, ritz_ref, last_ref, residual_ref, projected_ref, *, rows):
    form = jnp.zeros((ROWS, LANES), F32)
    for k in range(bits_ref.shape[0]):
        form += from_bits(bits_ref[k])
    inverse = inverse_ref[...]
    half = dot(inverse, unpack(form), 1, 0)
    projected = (dot(half, inverse, 1, 1) + dot(inverse, half, 1, 1)) * (1.0 / rows)
    projected_ref[...] = projected
    residual_ref[...] = last_ref[...] - dot(projected, ritz_ref[...], 0, 0)


def product(pairs, tiles, current, send_z):
    vectors, size = current.shape
    count = tiles.shape[0]
    y_count, z_count, xc_count = (lax.axis_size(Y), lax.axis_size(Z_LO), lax.axis_size(X_CORE))
    extra = send_z is not None
    if not extra:
        send_z = jnp.broadcast_to(current[None], (z_count, *current.shape))
    by_z = exchange(send_z, Z_LO)
    other = partner(current)
    column_block = spread(by_z, Y)
    send, direct = call(
        direct_kernel,
        ((xc_count, 4 * vectors + ROWS * extra, size), BF16),
        ((count, vectors, size), F32),
        scalars=1,
    )(pairs, column_block, tiles, current, other)
    arrived = exchange(send, X_CORE)
    send, own_direct, far = call(
        mirror_kernel,
        ((y_count, z_count, vectors, size), BF16),
        ((vectors, size), F32),
        ((vectors + 2 * ROWS * extra, size), BF16),
        scalars=1,
        scratch=[pltpu.VMEM((count, vectors, size), F32)],
    )(pairs, arrived, tiles, direct)
    mirror = exchange(send, Y)
    sent, far = (far, partner(far))
    if extra:
        mirror, gram = call(
            middle_kernel,
            ((z_count, vectors + ROWS, size), BF16),
            ((vectors, vectors), F32),
        )(mirror, sent, far)
    else:
        mirror, gram = (mirror.astype(F32).sum(axis=0).astype(BF16), None)
    mirror = exchange(mirror, Z_LO)
    return own_direct, far, mirror, gram


def steps(tile_values, tile_row, tile_col, basis_init):
    tiles = tile_values[0, 0]
    side = lax.axis_index(Z_HI).astype(jnp.int32)
    pairs = jnp.concatenate([tile_row[0, 0], tile_col[0, 0], side[None]])
    vectors, size = basis_init.shape
    total_rows = size * lax.axis_size(COL_ROW)

    own_direct, far, mirror, _ = product(pairs, tiles, basis_init, None)
    image, current, send = call(
        image_kernel,
        ((vectors, size), F32),
        ((vectors, size), BF16),
        ((mirror.shape[0], vectors + ROWS, size), BF16),
    )(own_direct, far, mirror)
    own_direct, far, mirror, gram = product(pairs, tiles, current, send)
    raw_image, send = call(
        last_kernel,
        ((vectors, size), F32),
        ((lax.axis_size(Y_X_CORE), ROWS, 2 * LANES), BF16),
    )(own_direct, far, mirror)
    form = exchange(send, Y_X_CORE)
    factor = jnp.linalg.cholesky(gram / total_rows)
    inverse = lax.linalg.triangular_solve(
        factor, jnp.eye(vectors, dtype=F32), left_side=True, lower=True
    )
    ritz_basis = jnp.dot(inverse, image, precision=HIGHEST)
    last_image = jnp.dot(inverse, raw_image, precision=HIGHEST)
    residual, projected = call(
        functools.partial(finish_kernel, rows=total_rows),
        ((vectors, size), F32),
        ((vectors, vectors), F32),
        out=jax.ShapeDtypeStruct,
    )(form, inverse, ritz_basis, last_image)
    return (ritz_basis, residual, projected)


def solution(mesh):
    finer = Mesh(mesh.devices.reshape(8, 4, 2, 4, 2), ("row_0", "row_1", "col_0", "col_1", "col_2"))
    placed = (P(ROW, COL, None, None, None), P(ROW, COL, None), P(ROW, COL, None), P(None, COL_ROW))
    return jax.shard_map(
        steps,
        mesh=finer,
        in_specs=placed,
        out_specs=(P(None, COL_ROW), P(None, COL_ROW), P()),
        check_vma=False,
    )
```

```python
import functools

import jax
import jax.numpy as jnp
from jax import lax
from jax.experimental import pallas as pl
from jax.experimental.pallas import tpu as pltpu
from jax.sharding import Mesh
from jax.sharding import PartitionSpec as P

Z_HI, X_CORE = ("col_0", ("col_1", "col_2"))
Z_LO, Y = ("row_0", "row_1")
Y_X_CORE = ("row_1", "col_1", "col_2")
COL = ("col_0", "col_1", "col_2")
ROW = ("row_0", "row_1")
COL_ROW = ("col_0", "col_1", "col_2", "row_0", "row_1")
HIGHEST = lax.Precision.HIGHEST
VMEM = pl.BlockSpec(memory_space=pltpu.VMEM)
SMEM = pl.BlockSpec(memory_space=pltpu.SMEM)
F32, BF16 = (jnp.float32, jnp.bfloat16)


def placed(value):
    return pltpu.with_memory_space_constraint(value, pltpu.VMEM)


ROWS, LANES, VECTORS = (8, 128, 32)


def exchange(parts, axis):
    return lax.all_to_all(parts, axis, 0, 0, tiled=True)


def call(kernel, *outs, scalars=0, scratch=(), out=pltpu.VMEM):
    def run(*args):
        args = args[:scalars] + tuple(placed(arg) for arg in args[scalars:])
        return pl.pallas_call(
            kernel,
            out_shape=tuple(out(shape, kind) for shape, kind in outs),
            in_specs=[SMEM] * scalars + [VMEM] * (len(args) - scalars),
            out_specs=tuple(VMEM for _ in outs),
            scratch_shapes=list(scratch),
        )(*args)

    return run


def partner(value):
    return lax.ppermute(value, Z_HI, [(0, 1), (1, 0)])


def pack(small):
    return jnp.concatenate([small[k : k + ROWS] for k in range(0, small.shape[0], ROWS)], axis=1)


def unpack(packed):
    return jnp.concatenate([packed[:, k : k + VECTORS] for k in range(0, LANES, VECTORS)], axis=0)


def from_bits(bits):
    wide = bits.astype(F32)
    return wide[..., LANES:] + wide[..., :LANES]


def dot(left, right, left_dim, right_dim):
    return lax.dot_general(
        left, right, (((left_dim,), (right_dim,)), ((), ())),
        precision=HIGHEST, preferred_element_type=F32,
    )


def store_bits(out_ref, place, packed):
    high = packed.astype(BF16)
    out_ref[(*place, slice(0, LANES))] = high
    out_ref[(*place, slice(LANES, 2 * LANES))] = (packed - high.astype(F32)).astype(BF16)


def store_sums(out_ref, slots, sums_ref):
    for t, (index, place) in enumerate(slots):
        total = sums_ref[t]
        for other, (other_index, _) in enumerate(slots):
            if other != t:
                total = total + (other_index == index).astype(F32) * sums_ref[other]
        out_ref[place] = total.astype(BF16)


def span(slot, length, start=0):
    if isinstance(slot, int):
        return pl.ds(start + slot * length, length)
    return pl.ds(pl.multiple_of(start + slot * length, length), length)


def spread_kernel(by_z_ref, note_ref, out_ref):
    length = by_z_ref.shape[1]
    for y in range(out_ref.shape[0]):
        for z in range(by_z_ref.shape[0]):
            out_ref[y, pl.ds(z * length, length)] = by_z_ref[z]
        out_ref[y, pl.ds(by_z_ref.shape[0] * length, ROWS)] = note_ref[...]


def select_kernel(peer_ref, by_z_ref, out_ref, *, vectors):
    y_count = out_ref.shape[0]
    tiles = peer_ref.shape[0] // y_count
    total = jnp.zeros((ROWS, LANES), F32)
    for z in range(by_z_ref.shape[0]):
        total += from_bits(by_z_ref[z, pl.ds(vectors, ROWS)])
    for y in range(y_count):
        for t in range(tiles):
            place = lax.div(peer_ref[y * tiles + t], y_count)
            out_ref[y, pl.ds(t * vectors, vectors)] = by_z_ref[place, pl.ds(0, vectors)]
        store_bits(out_ref, (y, pl.ds(tiles * vectors, ROWS)), total)


def direct_kernel(
    pair_ref, column_ref, tile_ref, own_ref, other_ref, out_ref, sums_ref, *, extra
):
    tiles, vectors = (tile_ref.shape[0], own_ref.shape[0])
    y_count, xc_count = (column_ref.shape[0], out_ref.shape[0])
    side = pair_ref[2 * tiles]
    for t in range(tiles):
        j = pair_ref[tiles + t]
        slot = t if extra else lax.div(j, y_count)
        from_column = column_ref[lax.rem(j, y_count), span(slot, vectors)]
        sums_ref[t] = lax.dot_general(
            from_column, tile_ref[t], (((1,), (1,)), ((), ())), preferred_element_type=F32
        )
    blank = jnp.zeros((2 * vectors, out_ref.shape[2]), BF16)
    for k in range(xc_count):
        out_ref[k, pl.ds(0, vectors)] = own_ref[...]
        out_ref[k, pl.ds(vectors, vectors)] = other_ref[...]
        out_ref[k, pl.ds(2 * vectors, 2 * vectors)] = blank
    if extra:
        total = jnp.zeros((ROWS, LANES), F32)
        for y in range(y_count):
            total += from_bits(column_ref[y, pl.ds(tiles * vectors, ROWS)])
        for k in range(xc_count):
            store_bits(out_ref, (k, pl.ds(4 * vectors, ROWS)), total)
    slots = []
    for t in range(tiles):
        i = pair_ref[t]
        half = lax.rem(lax.div(i, xc_count) + side, 2)
        slots.append((i, (lax.rem(i, xc_count), span(half, vectors, 2 * vectors))))
    store_sums(out_ref, slots, sums_ref)


def mirror_kernel(
    pair_ref, row_ref, tile_ref, direct_ref, out_ref, own_ref, far_ref, sums_ref
):
    tiles, vectors = (tile_ref.shape[0], own_ref.shape[0])
    y_count, xc_count = (out_ref.shape[0], row_ref.shape[0])
    extra = row_ref.shape[1] > 4 * vectors
    side = pair_ref[2 * tiles]
    form = jnp.zeros((vectors, vectors), F32)
    for t in range(tiles):
        i = pair_ref[t]
        half = lax.rem(lax.div(i, xc_count) + side, 2)
        from_row = row_ref[lax.rem(i, xc_count), span(half, vectors)]
        sums_ref[t] = jnp.dot(from_row, tile_ref[t], preferred_element_type=F32)
        if extra:
            form += dot(from_row.astype(F32), direct_ref[t], 1, 1)
    for s in range(2):
        rows = pl.ds((2 + s) * vectors, vectors)
        total = row_ref[0, rows].astype(F32)
        for k in range(1, xc_count):
            total = total + row_ref[k, rows].astype(F32)
        if s == 0:
            own_ref[...] = total
        else:
            far_ref[pl.ds(0, vectors)] = total.astype(BF16)
    if extra:
        total = jnp.zeros((ROWS, LANES), F32)
        for k in range(xc_count):
            total += from_bits(row_ref[k, pl.ds(4 * vectors, ROWS)])
        store_bits(far_ref, (pl.ds(vectors, ROWS),), total)
        store_bits(far_ref, (pl.ds(vectors + ROWS, ROWS),), pack(form))
    for k in range(y_count):
        out_ref[k] = jnp.zeros(out_ref.shape[1:], BF16)
    slots = []
    for t in range(tiles):
        j = pair_ref[tiles + t]
        slots.append((j, (lax.rem(j, y_count), lax.div(j, y_count))))
    store_sums(out_ref, slots, sums_ref)


def image_kernel(direct_ref, far_ref, mirror_ref, image_ref, current_ref, send_ref):
    image = direct_ref[...] + far_ref[...].astype(F32)
    for z in range(mirror_ref.shape[0]):
        image = image + mirror_ref[z].astype(F32)
    image_ref[...] = image
    current = image.astype(BF16)
    current_ref[...] = current
    gram = pack(dot(image, image, 1, 1))
    for z in range(send_ref.shape[0]):
        send_ref[z, pl.ds(0, image.shape[0])] = current
        store_bits(send_ref, (z, pl.ds(image.shape[0], ROWS)), gram)


def middle_kernel(mirror_ref, sent_ref, far_ref, send_ref, gram_ref):
    vectors = gram_ref.shape[0]
    for z in range(send_ref.shape[0]):
        total = mirror_ref[0, z].astype(F32)
        for y in range(1, mirror_ref.shape[0]):
            total = total + mirror_ref[y, z].astype(F32)
        send_ref[z, pl.ds(0, vectors)] = total.astype(BF16)
    rows = pl.ds(vectors, ROWS)
    gram_ref[...] = unpack(from_bits(sent_ref[rows]) + from_bits(far_ref[rows]))
    rows = pl.ds(vectors + ROWS, ROWS)
    form = from_bits(sent_ref[rows]) + from_bits(far_ref[rows])
    for z in range(send_ref.shape[0]):
        store_bits(send_ref, (z, pl.ds(vectors, ROWS)), form)


def last_kernel(direct_ref, far_ref, mirror_ref, image_ref, send_ref):
    vectors = image_ref.shape[0]
    form = jnp.zeros((ROWS, LANES), F32)
    for z in range(mirror_ref.shape[0]):
        form += from_bits(mirror_ref[z, pl.ds(vectors, ROWS)])
    for k in range(send_ref.shape[0]):
        store_bits(send_ref, (k, pl.ds(0, ROWS)), form)
    image = direct_ref[...] + far_ref[pl.ds(0, vectors)].astype(F32)
    for z in range(mirror_ref.shape[0]):
        image = image + mirror_ref[z, pl.ds(0, vectors)].astype(F32)
    image_ref[...] = image


def finish_kernel(bits_ref, inverse_ref, ritz_ref, last_ref, residual_ref, projected_ref, *, rows):
    form = jnp.zeros((ROWS, LANES), F32)
    for k in range(bits_ref.shape[0]):
        form += from_bits(bits_ref[k])
    inverse = inverse_ref[...]
    half = dot(inverse, unpack(form), 1, 0)
    projected = (dot(half, inverse, 1, 1) + dot(inverse, half, 1, 1)) * (1.0 / rows)
    projected_ref[...] = projected
    residual_ref[...] = last_ref[...] - dot(projected, ritz_ref[...], 0, 0)


def product(pairs, tiles, current, send_z, cols):
    vectors, size = current.shape
    count = tiles.shape[0]
    y_count, z_count, xc_count = (lax.axis_size(Y), lax.axis_size(Z_LO), lax.axis_size(X_CORE))
    extra = send_z is not None
    if not extra:
        send_z = placed(jnp.broadcast_to(current[None], (z_count, *current.shape)))
    by_z = exchange(send_z, Z_LO)
    other = partner(current)
    if extra:
        send = call(
            functools.partial(select_kernel, vectors=vectors),
            ((y_count, count * vectors + ROWS, size), BF16),
            scalars=1,
        )(cols, by_z)[0]
    else:
        note = jnp.pad(cols.astype(BF16)[None], [(0, ROWS - 1), (0, size - count)])
        send = call(
            spread_kernel, ((y_count, z_count * vectors + ROWS, size), BF16)
        )(by_z, note)[0]
    column_block = exchange(send, Y)
    if not extra:
        cols = column_block[:, z_count * vectors, :count].astype(jnp.int32).reshape(-1)
    send, direct = call(
        functools.partial(direct_kernel, extra=extra),
        ((xc_count, 4 * vectors + ROWS * extra, size), BF16),
        ((count, vectors, size), F32),
        scalars=1,
    )(pairs, column_block, tiles, current, other)
    arrived = exchange(send, X_CORE)
    send, own_direct, far = call(
        mirror_kernel,
        ((y_count, z_count, vectors, size), BF16),
        ((vectors, size), F32),
        ((vectors + 2 * ROWS * extra, size), BF16),
        scalars=1,
        scratch=[pltpu.VMEM((count, vectors, size), F32)],
    )(pairs, arrived, tiles, direct)
    mirror = exchange(send, Y)
    sent, far = (far, partner(far))
    if extra:
        mirror, gram = call(
            middle_kernel,
            ((z_count, vectors + ROWS, size), BF16),
            ((vectors, vectors), F32),
        )(mirror, sent, far)
    else:
        mirror, gram = (mirror.astype(F32).sum(axis=0).astype(BF16), None)
    mirror = exchange(mirror, Z_LO)
    return own_direct, far, mirror, gram, cols


def steps(tile_values, tile_row, tile_col, basis_init):
    tiles = tile_values[0, 0]
    side = lax.axis_index(Z_HI).astype(jnp.int32)
    pairs = jnp.concatenate([tile_row[0, 0], tile_col[0, 0], side[None]])
    vectors, size = basis_init.shape
    total_rows = size * lax.axis_size(COL_ROW)

    own_direct, far, mirror, _, cols = product(pairs, tiles, basis_init, None, tile_col[0, 0])
    image, current, send = call(
        image_kernel,
        ((vectors, size), F32),
        ((vectors, size), BF16),
        ((mirror.shape[0], vectors + ROWS, size), BF16),
    )(own_direct, far, mirror)
    own_direct, far, mirror, gram, _ = product(pairs, tiles, current, send, cols)
    raw_image, send = call(
        last_kernel,
        ((vectors, size), F32),
        ((lax.axis_size(Y_X_CORE), ROWS, 2 * LANES), BF16),
    )(own_direct, far, mirror)
    form = exchange(send, Y_X_CORE)
    factor = jnp.linalg.cholesky(gram / total_rows)
    inverse = lax.linalg.triangular_solve(
        factor, jnp.eye(vectors, dtype=F32), left_side=True, lower=True
    )
    ritz_basis = jnp.dot(inverse, image, precision=HIGHEST)
    last_image = jnp.dot(inverse, raw_image, precision=HIGHEST)
    residual, projected = call(
        functools.partial(finish_kernel, rows=total_rows),
        ((vectors, size), F32),
        ((vectors, vectors), F32),
        out=jax.ShapeDtypeStruct,
    )(form, inverse, ritz_basis, last_image)
    return (ritz_basis, residual, projected)


def solution(mesh):
    finer = Mesh(mesh.devices.reshape(8, 4, 2, 4, 2), ("row_0", "row_1", "col_0", "col_1", "col_2"))
    placed = (P(ROW, COL, None, None, None), P(ROW, COL, None), P(ROW, COL, None), P(None, COL_ROW))
    return jax.shard_map(
        steps,
        mesh=finer,
        in_specs=placed,
        out_specs=(P(None, COL_ROW), P(None, COL_ROW), P()),
        check_vma=False,
    )
```

```python
import functools

import jax
import jax.numpy as jnp
from jax import lax
from jax.experimental import pallas as pl
from jax.experimental.pallas import tpu as pltpu
from jax.sharding import Mesh
from jax.sharding import PartitionSpec as P

Z_HI, X_CORE = ("col_0", ("col_1", "col_2"))
Z_LO, Y = ("row_0", "row_1")
COL = ("col_0", "col_1", "col_2")
ROW = ("row_0", "row_1")
COL_ROW = ("col_0", "col_1", "col_2", "row_0", "row_1")
HIGHEST = lax.Precision.HIGHEST
VMEM = pl.BlockSpec(memory_space=pltpu.VMEM)
SMEM = pl.BlockSpec(memory_space=pltpu.SMEM)
F32, BF16 = (jnp.float32, jnp.bfloat16)


def placed(value):
    return pltpu.with_memory_space_constraint(value, pltpu.VMEM)


ROWS, LANES, VECTORS = (8, 128, 32)


def exchange(parts, axis):
    return lax.all_to_all(parts, axis, 0, 0, tiled=True)


def call(kernel, *outs, scalars=0, scratch=(), out=pltpu.VMEM):
    def run(*args):
        args = args[:scalars] + tuple(placed(arg) for arg in args[scalars:])
        return pl.pallas_call(
            kernel,
            out_shape=tuple(out(shape, kind) for shape, kind in outs),
            in_specs=[SMEM] * scalars + [VMEM] * (len(args) - scalars),
            out_specs=tuple(VMEM for _ in outs),
            scratch_shapes=list(scratch),
        )(*args)

    return run


def partner(value):
    return lax.ppermute(value, Z_HI, [(0, 1), (1, 0)])


def pack(small):
    return jnp.concatenate([small[k : k + ROWS] for k in range(0, small.shape[0], ROWS)], axis=1)


def unpack(packed):
    return jnp.concatenate([packed[:, k : k + VECTORS] for k in range(0, LANES, VECTORS)], axis=0)


def from_bits(bits):
    wide = bits.astype(F32)
    return wide[..., LANES:] + wide[..., :LANES]


def dot(left, right, left_dim, right_dim):
    return lax.dot_general(
        left, right, (((left_dim,), (right_dim,)), ((), ())),
        precision=HIGHEST, preferred_element_type=F32,
    )


def store_bits(out_ref, place, packed):
    high = packed.astype(BF16)
    out_ref[(*place, slice(0, LANES))] = high
    out_ref[(*place, slice(LANES, 2 * LANES))] = (packed - high.astype(F32)).astype(BF16)


def store_sums(out_ref, slots, sums_ref):
    for t, (index, place) in enumerate(slots):
        total = sums_ref[t]
        for other, (other_index, _) in enumerate(slots):
            if other != t:
                total = total + (other_index == index).astype(F32) * sums_ref[other]
        out_ref[place] = total.astype(BF16)


def parted(index, count):
    assert count & (count - 1) == 0
    return lax.shift_right_logical(index, count.bit_length() - 1), lax.bitwise_and(index, count - 1)


def span(slot, length, start=0):
    if isinstance(slot, int):
        return pl.ds(start + slot * length, length)
    return pl.ds(pl.multiple_of(start + slot * length, length), length)


def spread_kernel(by_z_ref, note_ref, out_ref):
    length = by_z_ref.shape[1]
    for y in range(out_ref.shape[0]):
        for z in range(by_z_ref.shape[0]):
            out_ref[y, pl.ds(z * length, length)] = by_z_ref[z]
        out_ref[y, pl.ds(by_z_ref.shape[0] * length, ROWS)] = note_ref[...]


def select_kernel(peer_ref, by_z_ref, out_ref, *, vectors):
    y_count = out_ref.shape[0]
    tiles = peer_ref.shape[0] // y_count
    total = jnp.zeros((ROWS, LANES), F32)
    for z in range(by_z_ref.shape[0]):
        total += from_bits(by_z_ref[z, pl.ds(vectors, ROWS)])
    for y in range(y_count):
        for t in range(tiles):
            place, _ = parted(peer_ref[y * tiles + t], y_count)
            out_ref[y, pl.ds(t * vectors, vectors)] = by_z_ref[place, pl.ds(0, vectors)]
        store_bits(out_ref, (y, pl.ds(tiles * vectors, ROWS)), total)


def direct_kernel(
    pair_ref, column_ref, tile_ref, own_ref, other_ref, out_ref, sums_ref, *, extra
):
    tiles, vectors = (tile_ref.shape[0], own_ref.shape[0])
    y_count, xc_count = (column_ref.shape[0], out_ref.shape[0])
    side = pair_ref[2 * tiles]
    for t in range(tiles):
        j = pair_ref[tiles + t]
        z, y = parted(j, y_count)
        from_column = column_ref[y, span(t if extra else z, vectors)]
        sums_ref[t] = lax.dot_general(
            from_column, tile_ref[t], (((1,), (1,)), ((), ())), preferred_element_type=F32
        )
    blank = jnp.zeros((2 * vectors, out_ref.shape[2]), BF16)
    for k in range(xc_count):
        out_ref[k, pl.ds(0, vectors)] = own_ref[...]
        out_ref[k, pl.ds(vectors, vectors)] = other_ref[...]
        out_ref[k, pl.ds(2 * vectors, 2 * vectors)] = blank
    if extra:
        total = jnp.zeros((ROWS, LANES), F32)
        for y in range(y_count):
            total += from_bits(column_ref[y, pl.ds(tiles * vectors, ROWS)])
        for k in range(xc_count):
            store_bits(out_ref, (k, pl.ds(4 * vectors, ROWS)), total)
    slots = []
    for t in range(tiles):
        i = pair_ref[t]
        half, xc = parted(i, xc_count)
        half = lax.bitwise_xor(half, side)
        slots.append((i, (xc, span(half, vectors, 2 * vectors))))
    store_sums(out_ref, slots, sums_ref)


def mirror_kernel(
    pair_ref, row_ref, tile_ref, direct_ref, out_ref, own_ref, far_ref, sums_ref
):
    tiles, vectors = (tile_ref.shape[0], own_ref.shape[0])
    y_count, xc_count = (out_ref.shape[0], row_ref.shape[0])
    extra = row_ref.shape[1] > 4 * vectors
    side = pair_ref[2 * tiles]
    form = jnp.zeros((vectors, vectors), F32)
    for t in range(tiles):
        i = pair_ref[t]
        half, xc = parted(i, xc_count)
        from_row = row_ref[xc, span(lax.bitwise_xor(half, side), vectors)]
        sums_ref[t] = jnp.dot(from_row, tile_ref[t], preferred_element_type=F32)
        if extra:
            form += dot(from_row.astype(F32), direct_ref[t], 1, 1)
    for s in range(2):
        rows = pl.ds((2 + s) * vectors, vectors)
        total = row_ref[0, rows].astype(F32)
        for k in range(1, xc_count):
            total = total + row_ref[k, rows].astype(F32)
        if s == 0:
            own_ref[...] = total
        else:
            far_ref[pl.ds(0, vectors)] = total.astype(BF16)
    if extra:
        total = jnp.zeros((ROWS, LANES), F32)
        for k in range(xc_count):
            total += from_bits(row_ref[k, pl.ds(4 * vectors, ROWS)])
        store_bits(far_ref, (pl.ds(vectors, ROWS),), total)
        packed = pack(form)
    length = out_ref.shape[1] - ROWS * extra
    for k in range(y_count):
        out_ref[k, pl.ds(0, length)] = jnp.zeros((length, out_ref.shape[2]), BF16)
        if extra:
            store_bits(out_ref, (k, pl.ds(length, ROWS)), packed)
    slots = []
    for t in range(tiles):
        j = pair_ref[tiles + t]
        z, y = parted(j, y_count)
        slots.append((j, (y, span(z, vectors))))
    store_sums(out_ref, slots, sums_ref)


def image_kernel(direct_ref, far_ref, mirror_ref, image_ref, current_ref, send_ref):
    image = direct_ref[...] + far_ref[...].astype(F32)
    for z in range(mirror_ref.shape[0]):
        image = image + mirror_ref[z].astype(F32)
    image_ref[...] = image
    current = image.astype(BF16)
    current_ref[...] = current
    gram = pack(dot(image, image, 1, 1))
    for z in range(send_ref.shape[0]):
        send_ref[z, pl.ds(0, image.shape[0])] = current
        store_bits(send_ref, (z, pl.ds(image.shape[0], ROWS)), gram)


def middle_kernel(mirror_ref, send_ref, *, vectors):
    z_count = send_ref.shape[0]
    for z in range(z_count):
        rows = pl.ds(z * vectors, vectors)
        total = mirror_ref[0, rows].astype(F32)
        for y in range(1, mirror_ref.shape[0]):
            total = total + mirror_ref[y, rows].astype(F32)
        send_ref[z, pl.ds(0, vectors)] = total.astype(BF16)
    if send_ref.shape[1] > vectors:
        form = jnp.zeros((ROWS, LANES), F32)
        for y in range(mirror_ref.shape[0]):
            form += from_bits(mirror_ref[y, pl.ds(z_count * vectors, ROWS)])
        for z in range(z_count):
            store_bits(send_ref, (z, pl.ds(vectors, ROWS)), form)


def gram_kernel(sent_ref, far_ref, gram_ref, *, rows):
    place = pl.ds(gram_ref.shape[0], ROWS)
    both = from_bits(sent_ref[place]) + from_bits(far_ref[place])
    gram_ref[...] = unpack(both) * (1.0 / rows)


def last_kernel(direct_ref, far_ref, mirror_ref, image_ref, send_ref):
    vectors = image_ref.shape[0]
    form = jnp.zeros((ROWS, LANES), F32)
    for z in range(mirror_ref.shape[0]):
        form += from_bits(mirror_ref[z, pl.ds(vectors, ROWS)])
    for k in range(send_ref.shape[0]):
        store_bits(send_ref, (k, pl.ds(0, ROWS)), form)
    image = direct_ref[...] + far_ref[pl.ds(0, vectors)].astype(F32)
    for z in range(mirror_ref.shape[0]):
        image = image + mirror_ref[z, pl.ds(0, vectors)].astype(F32)
    image_ref[...] = image


def finish_kernel(bits_ref, inverse_ref, ritz_ref, last_ref, residual_ref, projected_ref, *, rows):
    form = jnp.zeros((ROWS, LANES), F32)
    for k in range(bits_ref.shape[0]):
        form += from_bits(bits_ref[k])
    form = unpack(form)
    inverse = inverse_ref[...]
    half = dot(inverse, (form + form.T) * (1.0 / rows), 1, 0)
    projected_ref[...] = dot(half, inverse, 1, 1)
    residual_ref[...] = last_ref[...] - dot(half, ritz_ref[...], 1, 0)


def product(pairs, tiles, current, send_z, cols):
    vectors, size = current.shape
    count = tiles.shape[0]
    y_count, z_count, xc_count = (lax.axis_size(Y), lax.axis_size(Z_LO), lax.axis_size(X_CORE))
    extra = send_z is not None
    if not extra:
        send_z = placed(jnp.broadcast_to(current[None], (z_count, *current.shape)))
    by_z = exchange(send_z, Z_LO)
    other = partner(current)
    if extra:
        send = call(
            functools.partial(select_kernel, vectors=vectors),
            ((y_count, count * vectors + ROWS, size), BF16),
            scalars=1,
        )(cols, by_z)[0]
    else:
        note = jnp.pad(cols.astype(BF16)[None], [(0, ROWS - 1), (0, size - count)])
        send = call(
            spread_kernel, ((y_count, z_count * vectors + ROWS, size), BF16)
        )(by_z, note)[0]
    column_block = exchange(send, Y)
    if not extra:
        cols = column_block[:, z_count * vectors, :count].astype(jnp.int32).reshape(-1)
    send, direct = call(
        functools.partial(direct_kernel, extra=extra),
        ((xc_count, 4 * vectors + ROWS * extra, size), BF16),
        ((count, vectors, size), F32),
        scalars=1,
    )(pairs, column_block, tiles, current, other)
    arrived = exchange(send, X_CORE)
    send, own_direct, far = call(
        mirror_kernel,
        ((y_count, z_count * vectors + ROWS * extra, size), BF16),
        ((vectors, size), F32),
        ((vectors + ROWS * extra, size), BF16),
        scalars=1,
        scratch=[pltpu.VMEM((count, vectors, size), F32)],
    )(pairs, arrived, tiles, direct)
    mirror = exchange(send, Y)
    sent, far = (far, partner(far))
    mirror = call(
        functools.partial(middle_kernel, vectors=vectors),
        ((z_count, vectors + ROWS * extra, size), BF16),
    )(mirror)[0]
    mirror = exchange(mirror, Z_LO)
    return own_direct, sent, far, mirror, cols


def steps(tile_values, tile_row, tile_col, basis_init):
    tiles = tile_values[0, 0]
    side = lax.axis_index(Z_HI).astype(jnp.int32)
    pairs = jnp.concatenate([tile_row[0, 0], tile_col[0, 0], side[None]])
    vectors, size = basis_init.shape
    total_rows = size * lax.axis_size(COL_ROW)

    own_direct, _, far, mirror, cols = product(pairs, tiles, basis_init, None, tile_col[0, 0])
    image, current, send = call(
        image_kernel,
        ((vectors, size), F32),
        ((vectors, size), BF16),
        ((mirror.shape[0], vectors + ROWS, size), BF16),
    )(own_direct, far, mirror)
    own_direct, sent, far, mirror, _ = product(pairs, tiles, current, send, cols)
    raw_image, send = call(
        last_kernel,
        ((vectors, size), F32),
        ((lax.axis_size(COL), ROWS, 2 * LANES), BF16),
    )(own_direct, far, mirror)
    form = exchange(send, COL)
    gram = call(
        functools.partial(gram_kernel, rows=total_rows), ((vectors, vectors), F32)
    )(sent, far)[0]
    factor = jnp.linalg.cholesky(gram)
    inverse = lax.linalg.triangular_solve(
        factor, jnp.eye(vectors, dtype=F32), left_side=True, lower=True
    )
    ritz_basis = jnp.dot(inverse, image, precision=HIGHEST)
    last_image = jnp.dot(inverse, raw_image, precision=HIGHEST)
    turned = jnp.dot(inverse.T, ritz_basis, precision=HIGHEST)
    residual, projected = call(
        functools.partial(finish_kernel, rows=total_rows),
        ((vectors, size), F32),
        ((vectors, vectors), F32),
        out=jax.ShapeDtypeStruct,
    )(form, inverse, turned, last_image)
    return (ritz_basis, residual, projected)


def solution(mesh):
    finer = Mesh(mesh.devices.reshape(8, 4, 2, 4, 2), ("row_0", "row_1", "col_0", "col_1", "col_2"))
    placed = (P(ROW, COL, None, None, None), P(ROW, COL, None), P(ROW, COL, None), P(None, COL_ROW))
    return jax.shard_map(
        steps,
        mesh=finer,
        in_specs=placed,
        out_specs=(P(None, COL_ROW), P(None, COL_ROW), P()),
        check_vma=False,
    )
```

```python
import functools

import jax
import jax.numpy as jnp
from jax import lax
from jax.experimental import pallas as pl
from jax.experimental.pallas import tpu as pltpu
from jax.sharding import Mesh
from jax.sharding import PartitionSpec as P

Z_HI, X_CORE = ("col_0", ("col_1", "col_2"))
Z_LO, Y = ("row_0", "row_1")
Y_X_CORE = ("row_1", "col_1", "col_2")
COL = ("col_0", "col_1", "col_2")
ROW = ("row_0", "row_1")
COL_ROW = ("col_0", "col_1", "col_2", "row_0", "row_1")
HIGHEST = lax.Precision.HIGHEST
VMEM = pl.BlockSpec(memory_space=pltpu.VMEM)
SMEM = pl.BlockSpec(memory_space=pltpu.SMEM)
F32, BF16 = (jnp.float32, jnp.bfloat16)


def placed(value):
    return pltpu.with_memory_space_constraint(value, pltpu.VMEM)


ROWS, LANES, VECTORS = (8, 128, 32)


def exchange(parts, axis):
    return lax.all_to_all(parts, axis, 0, 0, tiled=True)


def call(kernel, *outs, scalars=0, scratch=(), out=pltpu.VMEM):
    def run(*args):
        args = args[:scalars] + tuple(placed(arg) for arg in args[scalars:])
        return pl.pallas_call(
            kernel,
            out_shape=tuple(out(shape, kind) for shape, kind in outs),
            in_specs=[SMEM] * scalars + [VMEM] * (len(args) - scalars),
            out_specs=tuple(VMEM for _ in outs),
            scratch_shapes=list(scratch),
        )(*args)

    return run


def partner(value):
    return lax.ppermute(value, Z_HI, [(0, 1), (1, 0)])


def pack(small):
    return jnp.concatenate([small[k : k + ROWS] for k in range(0, small.shape[0], ROWS)], axis=1)


def unpack(packed):
    return jnp.concatenate([packed[:, k : k + VECTORS] for k in range(0, LANES, VECTORS)], axis=0)


def from_bits(bits):
    wide = bits.astype(F32)
    return wide[..., LANES:] + wide[..., :LANES]


def dot(left, right, left_dim, right_dim):
    return lax.dot_general(
        left, right, (((left_dim,), (right_dim,)), ((), ())),
        precision=HIGHEST, preferred_element_type=F32,
    )


def store_bits(out_ref, place, packed):
    high = packed.astype(BF16)
    out_ref[(*place, slice(0, LANES))] = high
    out_ref[(*place, slice(LANES, 2 * LANES))] = (packed - high.astype(F32)).astype(BF16)


def store_sums(out_ref, slots, sums_ref):
    for t, (index, place) in enumerate(slots):
        total = sums_ref[t]
        for other, (other_index, _) in enumerate(slots):
            if other != t:
                total = total + (other_index == index).astype(F32) * sums_ref[other]
        out_ref[place] = total.astype(BF16)


def parted(index, count):
    assert count & (count - 1) == 0
    return lax.shift_right_logical(index, count.bit_length() - 1), lax.bitwise_and(index, count - 1)


def span(slot, length, start=0):
    if isinstance(slot, int):
        return pl.ds(start + slot * length, length)
    return pl.ds(pl.multiple_of(start + slot * length, length), length)


def select_kernel(peer_ref, by_z_ref, out_ref, *, vectors):
    y_count = out_ref.shape[0]
    tiles = peer_ref.shape[0] // y_count
    total = jnp.zeros((ROWS, LANES), F32)
    for z in range(by_z_ref.shape[0]):
        total += from_bits(by_z_ref[z, pl.ds(vectors, ROWS)])
    for y in range(y_count):
        for t in range(tiles):
            place, _ = parted(peer_ref[y * tiles + t], y_count)
            out_ref[y, pl.ds(t * vectors, vectors)] = by_z_ref[place, pl.ds(0, vectors)]
        store_bits(out_ref, (y, pl.ds(tiles * vectors, ROWS)), total)


def direct_kernel(
    pair_ref, column_ref, tile_ref, own_ref, other_ref, out_ref, sums_ref, *, extra
):
    tiles, vectors = (tile_ref.shape[0], own_ref.shape[0])
    y_count, xc_count = (column_ref.shape[0], out_ref.shape[0])
    side = pair_ref[2 * tiles]
    for t in range(tiles):
        j = pair_ref[tiles + t]
        if extra:
            from_column = column_ref[parted(j, y_count)[1], pl.ds(t * vectors, vectors)]
        else:
            from_column = column_ref[j]
        sums_ref[t] = lax.dot_general(
            from_column, tile_ref[t], (((1,), (1,)), ((), ())), preferred_element_type=F32
        )
    blank = jnp.zeros((2 * vectors, out_ref.shape[2]), BF16)
    for k in range(xc_count):
        out_ref[k, pl.ds(0, vectors)] = own_ref[...]
        out_ref[k, pl.ds(vectors, vectors)] = other_ref[...]
        out_ref[k, pl.ds(2 * vectors, 2 * vectors)] = blank
    if extra:
        total = jnp.zeros((ROWS, LANES), F32)
        for y in range(y_count):
            total += from_bits(column_ref[y, pl.ds(tiles * vectors, ROWS)])
        for k in range(xc_count):
            store_bits(out_ref, (k, pl.ds(4 * vectors, ROWS)), total)
    slots = []
    for t in range(tiles):
        i = pair_ref[t]
        half, xc = parted(i, xc_count)
        half = lax.bitwise_xor(half, side)
        slots.append((i, (xc, span(half, vectors, 2 * vectors))))
    store_sums(out_ref, slots, sums_ref)


def mirror_kernel(
    pair_ref, row_ref, tile_ref, near_ref, other_ref, out_ref, own_ref, far_ref, sums_ref
):
    tiles, vectors = (tile_ref.shape[0], own_ref.shape[0])
    y_count, xc_count = (out_ref.shape[0], row_ref.shape[0])
    extra = row_ref.shape[1] > 4 * vectors
    side = pair_ref[2 * tiles]
    for t in range(tiles):
        half, xc = parted(pair_ref[t], xc_count)
        from_row = row_ref[xc, span(lax.bitwise_xor(half, side), vectors)]
        sums_ref[t] = jnp.dot(from_row, tile_ref[t], preferred_element_type=F32)
    sums = []
    for s in range(2):
        rows = pl.ds((2 + s) * vectors, vectors)
        total = row_ref[0, rows].astype(F32)
        for k in range(1, xc_count):
            total = total + row_ref[k, rows].astype(F32)
        sums.append(total)
    own_ref[...] = sums[0]
    far_ref[pl.ds(0, vectors)] = sums[1].astype(BF16)
    if extra:
        total = jnp.zeros((ROWS, LANES), F32)
        for k in range(xc_count):
            total += from_bits(row_ref[k, pl.ds(4 * vectors, ROWS)])
        store_bits(far_ref, (pl.ds(vectors, ROWS),), total)
        form = dot(near_ref[...].astype(F32), sums[0], 1, 1)
        form += dot(other_ref[...].astype(F32), sums[1], 1, 1)
        store_bits(far_ref, (pl.ds(vectors + ROWS, ROWS),), pack(form))
    length = out_ref.shape[1] - ROWS * (not extra)
    for k in range(y_count):
        out_ref[k, pl.ds(0, length)] = jnp.zeros((length, out_ref.shape[2]), BF16)
        if not extra:
            out_ref[k, pl.ds(length, ROWS)] = other_ref[...]
    slots = []
    for t in range(tiles):
        j = pair_ref[tiles + t]
        z, y = parted(j, y_count)
        slots.append((j, (y, span(z, vectors))))
    store_sums(out_ref, slots, sums_ref)


def image_kernel(direct_ref, far_ref, mirror_ref, image_ref, current_ref, send_ref):
    image = direct_ref[...] + far_ref[...].astype(F32)
    for z in range(mirror_ref.shape[0]):
        image = image + mirror_ref[z].astype(F32)
    image_ref[...] = image
    current = image.astype(BF16)
    current_ref[...] = current
    gram = pack(dot(image, image, 1, 1))
    for z in range(send_ref.shape[0]):
        send_ref[z, pl.ds(0, image.shape[0])] = current
        store_bits(send_ref, (z, pl.ds(image.shape[0], ROWS)), gram)


def sum_over_y(mirror_ref, send_ref, vectors):
    for z in range(send_ref.shape[0]):
        rows = pl.ds(z * vectors, vectors)
        total = mirror_ref[0, rows].astype(F32)
        for y in range(1, mirror_ref.shape[0]):
            total = total + mirror_ref[y, rows].astype(F32)
        send_ref[z, pl.ds(0, vectors)] = total.astype(BF16)


def first_middle_kernel(mirror_ref, send_ref):
    sum_over_y(mirror_ref, send_ref, send_ref.shape[1])


def second_middle_kernel(mirror_ref, sent_ref, far_ref, send_ref, *, vectors):
    sum_over_y(mirror_ref, send_ref, vectors)
    rows = pl.ds(vectors + ROWS, ROWS)
    form = from_bits(sent_ref[rows]) + from_bits(far_ref[rows])
    for z in range(send_ref.shape[0]):
        store_bits(send_ref, (z, pl.ds(vectors, ROWS)), form)


def gram_kernel(sent_ref, far_ref, gram_ref, *, rows):
    place = pl.ds(gram_ref.shape[0], ROWS)
    both = from_bits(sent_ref[place]) + from_bits(far_ref[place])
    gram_ref[...] = unpack(both) * (1.0 / rows)


def last_kernel(direct_ref, far_ref, mirror_ref, image_ref, send_ref):
    vectors = image_ref.shape[0]
    form = jnp.zeros((ROWS, LANES), F32)
    for z in range(mirror_ref.shape[0]):
        form += from_bits(mirror_ref[z, pl.ds(vectors, ROWS)])
    for k in range(send_ref.shape[0]):
        store_bits(send_ref, (k, pl.ds(0, ROWS)), form)
    image = direct_ref[...] + far_ref[pl.ds(0, vectors)].astype(F32)
    for z in range(mirror_ref.shape[0]):
        image = image + mirror_ref[z, pl.ds(0, vectors)].astype(F32)
    image_ref[...] = image


def finish_kernel(bits_ref, inverse_ref, ritz_ref, last_ref, residual_ref, projected_ref, *, rows):
    form = jnp.zeros((ROWS, LANES), F32)
    for k in range(bits_ref.shape[0]):
        form += from_bits(bits_ref[k])
    form = unpack(form)
    inverse = inverse_ref[...]
    half = dot(inverse, (form + form.T) * (1.0 / rows), 1, 0)
    projected_ref[...] = dot(half, inverse, 1, 1)
    residual_ref[...] = last_ref[...] - dot(half, ritz_ref[...], 1, 0)


def product(pairs, tiles, current, send_z, note, peers):
    vectors, size = current.shape
    count = tiles.shape[0]
    y_count, z_count, xc_count = (lax.axis_size(Y), lax.axis_size(Z_LO), lax.axis_size(X_CORE))
    extra = send_z is not None
    if extra:
        by_z = exchange(send_z, Z_LO)
        other = partner(current)
        send = call(
            functools.partial(select_kernel, vectors=vectors),
            ((y_count, count * vectors + ROWS, size), BF16),
            scalars=1,
        )(peers, by_z)[0]
        column_block = exchange(send, Y)
    else:
        other = partner(current)
        row_count = lax.axis_size(ROW)
        send = jnp.broadcast_to(current[None], (row_count, vectors, size))
        column_block = exchange(send, ROW)
    send = call(
        functools.partial(direct_kernel, extra=extra),
        ((xc_count, 4 * vectors + ROWS * extra, size), BF16),
        scalars=1,
        scratch=[pltpu.VMEM((count, vectors, size), F32)],
    )(pairs, column_block, tiles, current, other)[0]
    arrived = exchange(send, X_CORE)
    send, own_direct, far = call(
        mirror_kernel,
        ((y_count, z_count * vectors + ROWS * (not extra), size), BF16),
        ((vectors, size), F32),
        ((vectors + 2 * ROWS * extra, size), BF16),
        scalars=1,
        scratch=[pltpu.VMEM((count, vectors, size), F32)],
    )(pairs, arrived, tiles, current, other if extra else note)
    mirror = exchange(send, Y)
    sent, far = (far, partner(far))
    out = ((z_count, vectors + ROWS * extra, size), BF16)
    if extra:
        middle = functools.partial(second_middle_kernel, vectors=vectors)
        mirror = call(middle, out)(mirror, sent, far)[0]
    else:
        peers = mirror[:, z_count * vectors, :count].astype(jnp.int32).reshape(-1)
        mirror = call(first_middle_kernel, out)(mirror)[0]
    mirror = exchange(mirror, Z_LO)
    return own_direct, sent, far, mirror, peers


def steps(tile_values, tile_row, tile_col, basis_init):
    tiles = tile_values[0, 0]
    side = lax.axis_index(Z_HI).astype(jnp.int32)
    pairs = jnp.concatenate([tile_row[0, 0], tile_col[0, 0], side[None]])
    vectors, size = basis_init.shape
    total_rows = size * lax.axis_size(COL_ROW)

    note = jnp.pad(
        tile_col[0].astype(BF16), [(0, ROWS - 1), (0, size - tiles.shape[0])]
    )
    own_direct, _, far, mirror, peers = product(pairs, tiles, basis_init, None, note, None)
    image, current, send = call(
        image_kernel,
        ((vectors, size), F32),
        ((vectors, size), BF16),
        ((mirror.shape[0], vectors + ROWS, size), BF16),
    )(own_direct, far, mirror)
    own_direct, sent, far, mirror, _ = product(pairs, tiles, current, send, None, peers)
    raw_image, send = call(
        last_kernel,
        ((vectors, size), F32),
        ((lax.axis_size(Y_X_CORE), ROWS, 2 * LANES), BF16),
    )(own_direct, far, mirror)
    form = exchange(send, Y_X_CORE)
    gram = call(
        functools.partial(gram_kernel, rows=total_rows), ((vectors, vectors), F32)
    )(sent, far)[0]
    factor = jnp.linalg.cholesky(gram)
    inverse = lax.linalg.triangular_solve(
        factor, jnp.eye(vectors, dtype=F32), left_side=True, lower=True
    )
    ritz_basis = jnp.dot(inverse, image, precision=HIGHEST)
    last_image = jnp.dot(inverse, raw_image, precision=HIGHEST)
    turned = jnp.dot(inverse.T, ritz_basis, precision=HIGHEST)
    residual, projected = call(
        functools.partial(finish_kernel, rows=total_rows),
        ((vectors, size), F32),
        ((vectors, vectors), F32),
        out=jax.ShapeDtypeStruct,
    )(form, inverse, turned, last_image)
    return (ritz_basis, residual, projected)


def solution(mesh):
    finer = Mesh(mesh.devices.reshape(8, 4, 2, 4, 2), ("row_0", "row_1", "col_0", "col_1", "col_2"))
    placed = (P(ROW, COL, None, None, None), P(ROW, COL, None), P(ROW, COL, None), P(None, COL_ROW))
    return jax.shard_map(
        steps,
        mesh=finer,
        in_specs=placed,
        out_specs=(P(None, COL_ROW), P(None, COL_ROW), P()),
        check_vma=False,
    )
```

```python
import functools

import jax
import jax.numpy as jnp
from jax import lax
from jax.experimental import pallas as pl
from jax.experimental.pallas import tpu as pltpu
from jax.sharding import Mesh
from jax.sharding import PartitionSpec as P

Z_HI, X_CORE = ("col_0", ("col_1", "col_2"))
Z_LO, Y = ("row_0", "row_1")
Y_X_CORE = ("row_1", "col_1", "col_2")
COL = ("col_0", "col_1", "col_2")
ROW = ("row_0", "row_1")
COL_ROW = ("col_0", "col_1", "col_2", "row_0", "row_1")
HIGHEST = lax.Precision.HIGHEST
VMEM = pl.BlockSpec(memory_space=pltpu.VMEM)
SMEM = pl.BlockSpec(memory_space=pltpu.SMEM)
F32, BF16 = (jnp.float32, jnp.bfloat16)


def placed(value):
    return pltpu.with_memory_space_constraint(value, pltpu.VMEM)


ROWS, LANES, VECTORS = (8, 128, 32)


def exchange(parts, axis):
    return lax.all_to_all(parts, axis, 0, 0, tiled=True)


def call(kernel, *outs, scalars=0, scratch=(), out=pltpu.VMEM):
    def run(*args):
        args = args[:scalars] + tuple(placed(arg) for arg in args[scalars:])
        return pl.pallas_call(
            kernel,
            out_shape=tuple(out(shape, kind) for shape, kind in outs),
            in_specs=[SMEM] * scalars + [VMEM] * (len(args) - scalars),
            out_specs=tuple(VMEM for _ in outs),
            scratch_shapes=list(scratch),
        )(*args)

    return run


def partner(value):
    return lax.ppermute(value, Z_HI, [(0, 1), (1, 0)])


def pack(small):
    return jnp.concatenate([small[k : k + ROWS] for k in range(0, small.shape[0], ROWS)], axis=1)


def unpack(packed):
    return jnp.concatenate([packed[:, k : k + VECTORS] for k in range(0, LANES, VECTORS)], axis=0)


def from_bits(bits):
    wide = bits.astype(F32)
    return wide[..., LANES:] + wide[..., :LANES]


def dot(left, right, left_dim, right_dim):
    return lax.dot_general(
        left, right, (((left_dim,), (right_dim,)), ((), ())),
        precision=HIGHEST, preferred_element_type=F32,
    )


def store_bits(out_ref, place, packed):
    high = packed.astype(BF16)
    out_ref[(*place, slice(0, LANES))] = high
    out_ref[(*place, slice(LANES, 2 * LANES))] = (packed - high.astype(F32)).astype(BF16)


def store_sums(out_ref, slots, sums_ref):
    for t, (index, place) in enumerate(slots):
        total = sums_ref[t]
        for other, (other_index, _) in enumerate(slots):
            if other != t:
                total = total + (other_index == index).astype(F32) * sums_ref[other]
        out_ref[place] = total.astype(BF16)


def parted(index, count):
    assert count & (count - 1) == 0
    return lax.shift_right_logical(index, count.bit_length() - 1), lax.bitwise_and(index, count - 1)


def span(slot, length, start=0):
    if isinstance(slot, int):
        return pl.ds(start + slot * length, length)
    return pl.ds(pl.multiple_of(start + slot * length, length), length)


def spread_kernel(by_z_ref, note_ref, out_ref):
    length = by_z_ref.shape[1]
    for y in range(out_ref.shape[0]):
        for z in range(by_z_ref.shape[0]):
            out_ref[y, pl.ds(z * length, length)] = by_z_ref[z]
        out_ref[y, pl.ds(by_z_ref.shape[0] * length, ROWS)] = note_ref[...]


def select_kernel(peer_ref, by_z_ref, out_ref, *, vectors):
    y_count = out_ref.shape[0]
    tiles = peer_ref.shape[0] // y_count
    total = jnp.zeros((ROWS, LANES), F32)
    for z in range(by_z_ref.shape[0]):
        total += from_bits(by_z_ref[z, pl.ds(vectors, ROWS)])
    for y in range(y_count):
        for t in range(tiles):
            place, _ = parted(peer_ref[y * tiles + t], y_count)
            out_ref[y, pl.ds(t * vectors, vectors)] = by_z_ref[place, pl.ds(0, vectors)]
        store_bits(out_ref, (y, pl.ds(tiles * vectors, ROWS)), total)


def direct_kernel(
    pair_ref, column_ref, tile_ref, own_ref, other_ref, out_ref, sums_ref, *, extra
):
    tiles, vectors = (tile_ref.shape[0], own_ref.shape[0])
    y_count, xc_count = (column_ref.shape[0], out_ref.shape[0])
    side = pair_ref[2 * tiles]
    for t in range(tiles):
        j = pair_ref[tiles + t]
        z, y = parted(j, y_count)
        from_column = column_ref[y, span(t if extra else z, vectors)]
        sums_ref[t] = lax.dot_general(
            from_column, tile_ref[t], (((1,), (1,)), ((), ())), preferred_element_type=F32
        )
    blank = jnp.zeros((2 * vectors, out_ref.shape[2]), BF16)
    for k in range(xc_count):
        out_ref[k, pl.ds(0, vectors)] = own_ref[...]
        out_ref[k, pl.ds(vectors, vectors)] = other_ref[...]
        out_ref[k, pl.ds(2 * vectors, 2 * vectors)] = blank
    if extra:
        total = jnp.zeros((ROWS, LANES), F32)
        for y in range(y_count):
            total += from_bits(column_ref[y, pl.ds(tiles * vectors, ROWS)])
        for k in range(xc_count):
            store_bits(out_ref, (k, pl.ds(4 * vectors, ROWS)), total)
    slots = []
    for t in range(tiles):
        i = pair_ref[t]
        half, xc = parted(i, xc_count)
        half = lax.bitwise_xor(half, side)
        slots.append((i, (xc, span(half, vectors, 2 * vectors))))
    store_sums(out_ref, slots, sums_ref)


def mirror_kernel(
    pair_ref, row_ref, tile_ref, near_ref, other_ref, out_ref, own_ref, far_ref, sums_ref
):
    tiles, vectors = (tile_ref.shape[0], own_ref.shape[0])
    y_count, xc_count = (out_ref.shape[0], row_ref.shape[0])
    extra = row_ref.shape[1] > 4 * vectors
    side = pair_ref[2 * tiles]
    for t in range(tiles):
        half, xc = parted(pair_ref[t], xc_count)
        from_row = row_ref[xc, span(lax.bitwise_xor(half, side), vectors)]
        sums_ref[t] = jnp.dot(from_row, tile_ref[t], preferred_element_type=F32)
    sums = []
    for s in range(2):
        rows = pl.ds((2 + s) * vectors, vectors)
        total = row_ref[0, rows].astype(F32)
        for k in range(1, xc_count):
            total = total + row_ref[k, rows].astype(F32)
        sums.append(total)
    own_ref[...] = sums[0]
    far_ref[pl.ds(0, vectors)] = sums[1].astype(BF16)
    if extra:
        total = jnp.zeros((ROWS, LANES), F32)
        for k in range(xc_count):
            total += from_bits(row_ref[k, pl.ds(4 * vectors, ROWS)])
        store_bits(far_ref, (pl.ds(vectors, ROWS),), total)
        form = dot(near_ref[...].astype(F32), sums[0], 1, 1)
        form += dot(other_ref[...].astype(F32), sums[1], 1, 1)
        store_bits(far_ref, (pl.ds(vectors + ROWS, ROWS),), pack(form))
    for k in range(y_count):
        out_ref[k] = jnp.zeros(out_ref.shape[1:], BF16)
    slots = []
    for t in range(tiles):
        j = pair_ref[tiles + t]
        z, y = parted(j, y_count)
        slots.append((j, (y, span(z, vectors))))
    store_sums(out_ref, slots, sums_ref)


def image_kernel(direct_ref, far_ref, mirror_ref, image_ref, current_ref, send_ref):
    image = direct_ref[...] + far_ref[...].astype(F32)
    for z in range(mirror_ref.shape[0]):
        image = image + mirror_ref[z].astype(F32)
    image_ref[...] = image
    current = image.astype(BF16)
    current_ref[...] = current
    gram = pack(dot(image, image, 1, 1))
    for z in range(send_ref.shape[0]):
        send_ref[z, pl.ds(0, image.shape[0])] = current
        store_bits(send_ref, (z, pl.ds(image.shape[0], ROWS)), gram)


def sum_over_y(mirror_ref, send_ref, vectors):
    for z in range(send_ref.shape[0]):
        rows = pl.ds(z * vectors, vectors)
        total = mirror_ref[0, rows].astype(F32)
        for y in range(1, mirror_ref.shape[0]):
            total = total + mirror_ref[y, rows].astype(F32)
        send_ref[z, pl.ds(0, vectors)] = total.astype(BF16)


def first_middle_kernel(mirror_ref, send_ref):
    sum_over_y(mirror_ref, send_ref, send_ref.shape[1])


def second_middle_kernel(mirror_ref, sent_ref, far_ref, send_ref, *, vectors):
    sum_over_y(mirror_ref, send_ref, vectors)
    rows = pl.ds(vectors + ROWS, ROWS)
    form = from_bits(sent_ref[rows]) + from_bits(far_ref[rows])
    for z in range(send_ref.shape[0]):
        store_bits(send_ref, (z, pl.ds(vectors, ROWS)), form)


def gram_kernel(sent_ref, far_ref, gram_ref, *, rows):
    place = pl.ds(gram_ref.shape[0], ROWS)
    both = from_bits(sent_ref[place]) + from_bits(far_ref[place])
    gram_ref[...] = unpack(both) * (1.0 / rows)


def last_kernel(direct_ref, far_ref, mirror_ref, image_ref, send_ref):
    vectors = image_ref.shape[0]
    form = jnp.zeros((ROWS, LANES), F32)
    for z in range(mirror_ref.shape[0]):
        form += from_bits(mirror_ref[z, pl.ds(vectors, ROWS)])
    for k in range(send_ref.shape[0]):
        store_bits(send_ref, (k, pl.ds(0, ROWS)), form)
    image = direct_ref[...] + far_ref[pl.ds(0, vectors)].astype(F32)
    for z in range(mirror_ref.shape[0]):
        image = image + mirror_ref[z, pl.ds(0, vectors)].astype(F32)
    image_ref[...] = image


def finish_kernel(bits_ref, inverse_ref, ritz_ref, last_ref, residual_ref, projected_ref, *, rows):
    form = jnp.zeros((ROWS, LANES), F32)
    for k in range(bits_ref.shape[0]):
        form += from_bits(bits_ref[k])
    form = unpack(form)
    inverse = inverse_ref[...]
    half = dot(inverse, (form + form.T) * (1.0 / rows), 1, 0)
    projected_ref[...] = dot(half, inverse, 1, 1)
    residual_ref[...] = last_ref[...] - dot(half, ritz_ref[...], 1, 0)


def product(pairs, tiles, current, send_z, note, peers):
    vectors, size = current.shape
    count = tiles.shape[0]
    y_count, z_count, xc_count = (lax.axis_size(Y), lax.axis_size(Z_LO), lax.axis_size(X_CORE))
    extra = send_z is not None
    if not extra:
        send_z = jnp.broadcast_to(current[None], (z_count, vectors, size))
    by_z = exchange(send_z, Z_LO)
    other = partner(current)
    if extra:
        select = functools.partial(select_kernel, vectors=vectors)
        out = ((y_count, count * vectors + ROWS, size), BF16)
        send = call(select, out, scalars=1)(peers, by_z)[0]
    else:
        out = ((y_count, z_count * vectors + ROWS, size), BF16)
        send = call(spread_kernel, out)(by_z, note)[0]
    column_block = exchange(send, Y)
    if not extra:
        peers = column_block[:, z_count * vectors, :count].astype(jnp.int32).reshape(-1)
    send = call(
        functools.partial(direct_kernel, extra=extra),
        ((xc_count, 4 * vectors + ROWS * extra, size), BF16),
        scalars=1,
        scratch=[pltpu.VMEM((count, vectors, size), F32)],
    )(pairs, column_block, tiles, current, other)[0]
    arrived = exchange(send, X_CORE)
    send, own_direct, far = call(
        mirror_kernel,
        ((y_count, z_count * vectors, size), BF16),
        ((vectors, size), F32),
        ((vectors + 2 * ROWS * extra, size), BF16),
        scalars=1,
        scratch=[pltpu.VMEM((count, vectors, size), F32)],
    )(pairs, arrived, tiles, current, other)
    mirror = exchange(send, Y)
    sent, far = (far, partner(far))
    out = ((z_count, vectors + ROWS * extra, size), BF16)
    if extra:
        middle = functools.partial(second_middle_kernel, vectors=vectors)
        mirror = call(middle, out)(mirror, sent, far)[0]
    else:
        mirror = call(first_middle_kernel, out)(mirror)[0]
    mirror = exchange(mirror, Z_LO)
    return own_direct, sent, far, mirror, peers


def steps(tile_values, tile_row, tile_col, basis_init):
    tiles = tile_values[0, 0]
    side = lax.axis_index(Z_HI).astype(jnp.int32)
    pairs = jnp.concatenate([tile_row[0, 0], tile_col[0, 0], side[None]])
    vectors, size = basis_init.shape
    total_rows = size * lax.axis_size(COL_ROW)

    note = jnp.pad(
        tile_col[0].astype(BF16), [(0, ROWS - 1), (0, size - tiles.shape[0])]
    )
    own_direct, _, far, mirror, peers = product(pairs, tiles, basis_init, None, note, None)
    image, current, send = call(
        image_kernel,
        ((vectors, size), F32),
        ((vectors, size), BF16),
        ((mirror.shape[0], vectors + ROWS, size), BF16),
    )(own_direct, far, mirror)
    own_direct, sent, far, mirror, _ = product(pairs, tiles, current, send, None, peers)
    raw_image, send = call(
        last_kernel,
        ((vectors, size), F32),
        ((lax.axis_size(Y_X_CORE), ROWS, 2 * LANES), BF16),
    )(own_direct, far, mirror)
    form = exchange(send, Y_X_CORE)
    gram = call(
        functools.partial(gram_kernel, rows=total_rows), ((vectors, vectors), F32)
    )(sent, far)[0]
    factor = jnp.linalg.cholesky(gram)
    inverse = lax.linalg.triangular_solve(
        factor, jnp.eye(vectors, dtype=F32), left_side=True, lower=True
    )
    ritz_basis = jnp.dot(inverse, image, precision=HIGHEST)
    last_image = jnp.dot(inverse, raw_image, precision=HIGHEST)
    turned = jnp.dot(inverse.T, ritz_basis, precision=HIGHEST)
    residual, projected = call(
        functools.partial(finish_kernel, rows=total_rows),
        ((vectors, size), F32),
        ((vectors, vectors), F32),
        out=jax.ShapeDtypeStruct,
    )(form, inverse, turned, last_image)
    return (ritz_basis, residual, projected)


def solution(mesh):
    finer = Mesh(mesh.devices.reshape(8, 4, 2, 4, 2), ("row_0", "row_1", "col_0", "col_1", "col_2"))
    placed = (P(ROW, COL, None, None, None), P(ROW, COL, None), P(ROW, COL, None), P(None, COL_ROW))
    return jax.shard_map(
        steps,
        mesh=finer,
        in_specs=placed,
        out_specs=(P(None, COL_ROW), P(None, COL_ROW), P()),
        check_vma=False,
    )
```

```python
import functools

import jax
import jax.numpy as jnp
from jax import lax
from jax.experimental import pallas as pl
from jax.experimental.pallas import tpu as pltpu
from jax.sharding import Mesh
from jax.sharding import PartitionSpec as P

Z_HI, X_CORE = ("col_0", ("col_1", "col_2"))
Z_LO, Y = ("row_0", "row_1")
Y_X_CORE = ("row_1", "col_1", "col_2")
COL = ("col_0", "col_1", "col_2")
ROW = ("row_0", "row_1")
COL_ROW = ("col_0", "col_1", "col_2", "row_0", "row_1")
HIGHEST = lax.Precision.HIGHEST
VMEM = pl.BlockSpec(memory_space=pltpu.VMEM)
F32, BF16 = (jnp.float32, jnp.bfloat16)


def placed(value):
    return pltpu.with_memory_space_constraint(value, pltpu.VMEM)


ROWS, LANES, VECTORS = (8, 128, 32)


def exchange(parts, axis):
    return lax.all_to_all(parts, axis, 0, 0, tiled=True)


def call(kernel, *outs, scratch=(), out=pltpu.VMEM):
    def run(*args):
        args = tuple(placed(arg) for arg in args)
        return pl.pallas_call(
            kernel,
            out_shape=tuple(out(shape, kind) for shape, kind in outs),
            in_specs=[VMEM] * len(args),
            out_specs=tuple(VMEM for _ in outs),
            scratch_shapes=list(scratch),
        )(*args)

    return run


def partner(value):
    return lax.ppermute(value, Z_HI, [(0, 1), (1, 0)])


def pack(small):
    return jnp.concatenate([small[k : k + ROWS] for k in range(0, small.shape[0], ROWS)], axis=1)


def unpack(packed):
    return jnp.concatenate([packed[:, k : k + VECTORS] for k in range(0, LANES, VECTORS)], axis=0)


def from_bits(bits):
    wide = bits.astype(F32)
    return wide[..., LANES:] + wide[..., :LANES]


def dot(left, right, left_dim, right_dim):
    return lax.dot_general(
        left, right, (((left_dim,), (right_dim,)), ((), ())),
        precision=HIGHEST, preferred_element_type=F32,
    )


def store_bits(out_ref, place, packed):
    high = packed.astype(BF16)
    out_ref[(*place, slice(0, LANES))] = high
    out_ref[(*place, slice(LANES, 2 * LANES))] = (packed - high.astype(F32)).astype(BF16)


def store_sums(out_ref, slots, sums_ref):
    for t, (index, place) in enumerate(slots):
        total = sums_ref[t]
        for other, (other_index, _) in enumerate(slots):
            if other != t:
                total = total + (other_index == index).astype(F32) * sums_ref[other]
        out_ref[place] = total.astype(BF16)


def parted(index, count):
    assert count & (count - 1) == 0
    return lax.shift_right_logical(index, count.bit_length() - 1), lax.bitwise_and(index, count - 1)


def span(slot, length, start=0):
    if isinstance(slot, int):
        return pl.ds(start + slot * length, length)
    return pl.ds(pl.multiple_of(start + slot * length, length), length)


def spread_kernel(by_z_ref, note_ref, out_ref):
    length = by_z_ref.shape[1]
    for y in range(out_ref.shape[0]):
        for z in range(by_z_ref.shape[0]):
            out_ref[y, pl.ds(z * length, length)] = by_z_ref[z]
        out_ref[y, pl.ds(by_z_ref.shape[0] * length, ROWS)] = note_ref[...]


def select_kernel(peer_ref, by_z_ref, out_ref, *, vectors):
    y_count = out_ref.shape[0]
    tiles = (out_ref.shape[1] - ROWS) // vectors
    total = jnp.zeros((ROWS, LANES), F32)
    for z in range(by_z_ref.shape[0]):
        total += from_bits(by_z_ref[z, pl.ds(vectors, ROWS)])
    for y in range(y_count):
        for t in range(tiles):
            place, _ = parted(peer_ref[y, t], y_count)
            out_ref[y, pl.ds(t * vectors, vectors)] = by_z_ref[place, pl.ds(0, vectors)]
        store_bits(out_ref, (y, pl.ds(tiles * vectors, ROWS)), total)


def direct_kernel(
    pair_ref, column_ref, tile_ref, own_ref, other_ref, out_ref, sums_ref, *, extra
):
    tiles, vectors = (tile_ref.shape[0], own_ref.shape[0])
    y_count, xc_count = (column_ref.shape[0], out_ref.shape[0])
    side = pair_ref[0, 2 * tiles]
    for t in range(tiles):
        j = pair_ref[0, tiles + t]
        z, y = parted(j, y_count)
        from_column = column_ref[y, span(t if extra else z, vectors)]
        sums_ref[t] = lax.dot_general(
            from_column, tile_ref[t], (((1,), (1,)), ((), ())), preferred_element_type=F32
        )
    blank = jnp.zeros((2 * vectors, out_ref.shape[2]), BF16)
    for k in range(xc_count):
        out_ref[k, pl.ds(0, vectors)] = own_ref[...]
        out_ref[k, pl.ds(vectors, vectors)] = other_ref[...]
        out_ref[k, pl.ds(2 * vectors, 2 * vectors)] = blank
    if extra:
        total = jnp.zeros((ROWS, LANES), F32)
        for y in range(y_count):
            total += from_bits(column_ref[y, pl.ds(tiles * vectors, ROWS)])
        for k in range(xc_count):
            store_bits(out_ref, (k, pl.ds(4 * vectors, ROWS)), total)
    slots = []
    for t in range(tiles):
        i = pair_ref[0, t]
        half, xc = parted(i, xc_count)
        half = lax.bitwise_xor(half, side)
        slots.append((i, (xc, span(half, vectors, 2 * vectors))))
    store_sums(out_ref, slots, sums_ref)


def mirror_kernel(
    pair_ref, row_ref, tile_ref, near_ref, other_ref, out_ref, own_ref, far_ref, sums_ref
):
    tiles, vectors = (tile_ref.shape[0], own_ref.shape[0])
    y_count, xc_count = (out_ref.shape[0], row_ref.shape[0])
    extra = row_ref.shape[1] > 4 * vectors
    side = pair_ref[0, 2 * tiles]
    for t in range(tiles):
        half, xc = parted(pair_ref[0, t], xc_count)
        from_row = row_ref[xc, span(lax.bitwise_xor(half, side), vectors)]
        sums_ref[t] = jnp.dot(from_row, tile_ref[t], preferred_element_type=F32)
    sums = []
    for s in range(2):
        rows = pl.ds((2 + s) * vectors, vectors)
        total = row_ref[0, rows].astype(F32)
        for k in range(1, xc_count):
            total = total + row_ref[k, rows].astype(F32)
        sums.append(total)
    own_ref[...] = sums[0]
    far_ref[pl.ds(0, vectors)] = sums[1].astype(BF16)
    if extra:
        total = jnp.zeros((ROWS, LANES), F32)
        for k in range(xc_count):
            total += from_bits(row_ref[k, pl.ds(4 * vectors, ROWS)])
        store_bits(far_ref, (pl.ds(vectors, ROWS),), total)
        form = dot(near_ref[...].astype(F32), sums[0], 1, 1)
        form += dot(other_ref[...].astype(F32), sums[1], 1, 1)
        store_bits(far_ref, (pl.ds(vectors + ROWS, ROWS),), pack(form))
    for k in range(y_count):
        out_ref[k] = jnp.zeros(out_ref.shape[1:], BF16)
    slots = []
    for t in range(tiles):
        j = pair_ref[0, tiles + t]
        z, y = parted(j, y_count)
        slots.append((j, (y, span(z, vectors))))
    store_sums(out_ref, slots, sums_ref)


def image_kernel(direct_ref, far_ref, mirror_ref, image_ref, current_ref, send_ref):
    image = direct_ref[...] + far_ref[...].astype(F32)
    for z in range(mirror_ref.shape[0]):
        image = image + mirror_ref[z].astype(F32)
    image_ref[...] = image
    current = image.astype(BF16)
    current_ref[...] = current
    gram = pack(dot(image, image, 1, 1))
    for z in range(send_ref.shape[0]):
        send_ref[z, pl.ds(0, image.shape[0])] = current
        store_bits(send_ref, (z, pl.ds(image.shape[0], ROWS)), gram)


def sum_over_y(mirror_ref, send_ref, vectors):
    for z in range(send_ref.shape[0]):
        rows = pl.ds(z * vectors, vectors)
        total = mirror_ref[0, rows].astype(F32)
        for y in range(1, mirror_ref.shape[0]):
            total = total + mirror_ref[y, rows].astype(F32)
        send_ref[z, pl.ds(0, vectors)] = total.astype(BF16)


def first_middle_kernel(mirror_ref, send_ref):
    sum_over_y(mirror_ref, send_ref, send_ref.shape[1])


def second_middle_kernel(mirror_ref, sent_ref, far_ref, send_ref, *, vectors):
    sum_over_y(mirror_ref, send_ref, vectors)
    rows = pl.ds(vectors + ROWS, ROWS)
    form = from_bits(sent_ref[rows]) + from_bits(far_ref[rows])
    for z in range(send_ref.shape[0]):
        store_bits(send_ref, (z, pl.ds(vectors, ROWS)), form)


def gram_kernel(sent_ref, far_ref, gram_ref, *, rows):
    place = pl.ds(gram_ref.shape[0], ROWS)
    both = from_bits(sent_ref[place]) + from_bits(far_ref[place])
    gram_ref[...] = unpack(both) * (1.0 / rows)


def last_kernel(direct_ref, far_ref, mirror_ref, image_ref, send_ref):
    vectors = image_ref.shape[0]
    form = jnp.zeros((ROWS, LANES), F32)
    for z in range(mirror_ref.shape[0]):
        form += from_bits(mirror_ref[z, pl.ds(vectors, ROWS)])
    for k in range(send_ref.shape[0]):
        store_bits(send_ref, (k, pl.ds(0, ROWS)), form)
    image = direct_ref[...] + far_ref[pl.ds(0, vectors)].astype(F32)
    for z in range(mirror_ref.shape[0]):
        image = image + mirror_ref[z, pl.ds(0, vectors)].astype(F32)
    image_ref[...] = image


def finish_kernel(bits_ref, inverse_ref, ritz_ref, last_ref, residual_ref, projected_ref, *, rows):
    form = jnp.zeros((ROWS, LANES), F32)
    for k in range(bits_ref.shape[0]):
        form += from_bits(bits_ref[k])
    form = unpack(form)
    inverse = inverse_ref[...]
    half = dot(inverse, (form + form.T) * (1.0 / rows), 1, 0)
    projected_ref[...] = dot(half, inverse, 1, 1)
    residual_ref[...] = last_ref[...] - dot(half, ritz_ref[...], 1, 0)


def product(pairs, tiles, current, send_z, note, peers):
    vectors, size = current.shape
    count = tiles.shape[0]
    y_count, z_count, xc_count = (lax.axis_size(Y), lax.axis_size(Z_LO), lax.axis_size(X_CORE))
    extra = send_z is not None
    if not extra:
        send_z = jnp.broadcast_to(current[None], (z_count, vectors, size))
    by_z = exchange(send_z, Z_LO)
    other = partner(current)
    if extra:
        select = functools.partial(select_kernel, vectors=vectors)
        out = ((y_count, count * vectors + ROWS, size), BF16)
        send = call(select, out)(peers, by_z)[0]
    else:
        out = ((y_count, z_count * vectors + ROWS, size), BF16)
        send = call(spread_kernel, out)(by_z, note)[0]
    column_block = exchange(send, Y)
    if not extra:
        peers = column_block[:, z_count * vectors, :LANES].astype(jnp.int32)
    send = call(
        functools.partial(direct_kernel, extra=extra),
        ((xc_count, 4 * vectors + ROWS * extra, size), BF16),
        scratch=[pltpu.VMEM((count, vectors, size), F32)],
    )(pairs, column_block, tiles, current, other)[0]
    arrived = exchange(send, X_CORE)
    send, own_direct, far = call(
        mirror_kernel,
        ((y_count, z_count * vectors, size), BF16),
        ((vectors, size), F32),
        ((vectors + 2 * ROWS * extra, size), BF16),
        scratch=[pltpu.VMEM((count, vectors, size), F32)],
    )(pairs, arrived, tiles, current, other)
    mirror = exchange(send, Y)
    sent, far = (far, partner(far))
    out = ((z_count, vectors + ROWS * extra, size), BF16)
    if extra:
        middle = functools.partial(second_middle_kernel, vectors=vectors)
        mirror = call(middle, out)(mirror, sent, far)[0]
    else:
        mirror = call(first_middle_kernel, out)(mirror)[0]
    mirror = exchange(mirror, Z_LO)
    return own_direct, sent, far, mirror, peers


def steps(tile_values, tile_row, tile_col, basis_init):
    tiles = tile_values[0, 0]
    side = lax.axis_index(Z_HI).astype(jnp.int32)
    pairs = jnp.concatenate([tile_row[0], tile_col[0], side[None, None]], axis=1)
    pairs = jnp.pad(pairs, [(0, 0), (0, LANES - pairs.shape[1])])
    vectors, size = basis_init.shape
    total_rows = size * lax.axis_size(COL_ROW)

    note = jnp.pad(
        tile_col[0].astype(BF16), [(0, ROWS - 1), (0, size - tiles.shape[0])]
    )
    own_direct, _, far, mirror, peers = product(pairs, tiles, basis_init, None, note, None)
    image, current, send = call(
        image_kernel,
        ((vectors, size), F32),
        ((vectors, size), BF16),
        ((mirror.shape[0], vectors + ROWS, size), BF16),
    )(own_direct, far, mirror)
    own_direct, sent, far, mirror, _ = product(pairs, tiles, current, send, None, peers)
    raw_image, send = call(
        last_kernel,
        ((vectors, size), F32),
        ((lax.axis_size(Y_X_CORE), ROWS, 2 * LANES), BF16),
    )(own_direct, far, mirror)
    form = exchange(send, Y_X_CORE)
    gram = call(
        functools.partial(gram_kernel, rows=total_rows), ((vectors, vectors), F32)
    )(sent, far)[0]
    factor = jnp.linalg.cholesky(gram)
    inverse = lax.linalg.triangular_solve(
        factor, jnp.eye(vectors, dtype=F32), left_side=True, lower=True
    )
    ritz_basis = jnp.dot(inverse, image, precision=HIGHEST)
    last_image = jnp.dot(inverse, raw_image, precision=HIGHEST)
    turned = jnp.dot(inverse.T, ritz_basis, precision=HIGHEST)
    residual, projected = call(
        functools.partial(finish_kernel, rows=total_rows),
        ((vectors, size), F32),
        ((vectors, vectors), F32),
        out=jax.ShapeDtypeStruct,
    )(form, inverse, turned, last_image)
    return (ritz_basis, residual, projected)


def solution(mesh):
    finer = Mesh(mesh.devices.reshape(8, 4, 2, 4, 2), ("row_0", "row_1", "col_0", "col_1", "col_2"))
    placed = (P(ROW, COL, None, None, None), P(ROW, COL, None), P(ROW, COL, None), P(None, COL_ROW))
    return jax.shard_map(
        steps,
        mesh=finer,
        in_specs=placed,
        out_specs=(P(None, COL_ROW), P(None, COL_ROW), P()),
        check_vma=False,
    )
```

```python
import functools

import jax
import jax.numpy as jnp
from jax import lax
from jax.experimental import pallas as pl
from jax.experimental.pallas import tpu as pltpu
from jax.sharding import Mesh
from jax.sharding import PartitionSpec as P

Z_HI, X_CORE = ("col_0", ("col_1", "col_2"))
Z_LO, Y = ("row_0", "row_1")
Y_X_CORE = ("row_1", "col_1", "col_2")
COL = ("col_0", "col_1", "col_2")
ROW = ("row_0", "row_1")
COL_ROW = ("col_0", "col_1", "col_2", "row_0", "row_1")
HIGHEST = lax.Precision.HIGHEST
VMEM = pl.BlockSpec(memory_space=pltpu.VMEM)
F32, BF16 = (jnp.float32, jnp.bfloat16)


def placed(value):
    return pltpu.with_memory_space_constraint(value, pltpu.VMEM)


ROWS, LANES, VECTORS = (8, 128, 32)


def exchange(parts, axis):
    return lax.all_to_all(parts, axis, 0, 0, tiled=True)


def call(kernel, *outs, scratch=(), out=pltpu.VMEM):
    def run(*args):
        args = tuple(placed(arg) for arg in args)
        return pl.pallas_call(
            kernel,
            out_shape=tuple(out(shape, kind) for shape, kind in outs),
            in_specs=[VMEM] * len(args),
            out_specs=tuple(VMEM for _ in outs),
            scratch_shapes=list(scratch),
        )(*args)

    return run


def partner(value):
    return lax.ppermute(value, Z_HI, [(0, 1), (1, 0)])


def pack(small):
    return jnp.concatenate([small[k : k + ROWS] for k in range(0, small.shape[0], ROWS)], axis=1)


def unpack(packed):
    return jnp.concatenate([packed[:, k : k + VECTORS] for k in range(0, LANES, VECTORS)], axis=0)


def from_bits(bits):
    wide = bits.astype(F32)
    return wide[..., LANES:] + wide[..., :LANES]


def dot(left, right, left_dim, right_dim):
    return lax.dot_general(
        left, right, (((left_dim,), (right_dim,)), ((), ())),
        precision=HIGHEST, preferred_element_type=F32,
    )


def store_bits(out_ref, place, packed):
    high = packed.astype(BF16)
    out_ref[(*place, slice(0, LANES))] = high
    out_ref[(*place, slice(LANES, 2 * LANES))] = (packed - high.astype(F32)).astype(BF16)


def store_sums(out_ref, slots, sums_ref):
    for t, (index, place) in enumerate(slots):
        total = sums_ref[t]
        for other, (other_index, _) in enumerate(slots):
            if other != t:
                total = total + (other_index == index).astype(F32) * sums_ref[other]
        out_ref[place] = total.astype(BF16)


def parted(index, count):
    assert count & (count - 1) == 0
    return lax.shift_right_logical(index, count.bit_length() - 1), lax.bitwise_and(index, count - 1)


def span(slot, length, start=0):
    if isinstance(slot, int):
        return pl.ds(start + slot * length, length)
    return pl.ds(pl.multiple_of(start + slot * length, length), length)


def spread_kernel(by_z_ref, note_ref, out_ref):
    length = by_z_ref.shape[1]
    for y in range(out_ref.shape[0]):
        for z in range(by_z_ref.shape[0]):
            out_ref[y, pl.ds(z * length, length)] = by_z_ref[z]
        out_ref[y, pl.ds(by_z_ref.shape[0] * length, ROWS)] = note_ref[...]


def select_kernel(peer_ref, by_z_ref, out_ref, *, vectors):
    y_count = out_ref.shape[0]
    tiles = (out_ref.shape[1] - ROWS) // vectors
    total = jnp.zeros((ROWS, LANES), F32)
    for z in range(by_z_ref.shape[0]):
        total += from_bits(by_z_ref[z, pl.ds(vectors, ROWS)])
    for y in range(y_count):
        for t in range(tiles):
            place, _ = parted(peer_ref[y, t], y_count)
            out_ref[y, pl.ds(t * vectors, vectors)] = by_z_ref[place, pl.ds(0, vectors)]
        store_bits(out_ref, (y, pl.ds(tiles * vectors, ROWS)), total)


def direct_kernel(
    pair_ref, column_ref, tile_ref, own_ref, other_ref, out_ref, sums_ref, *, extra
):
    tiles, vectors = (tile_ref.shape[0], own_ref.shape[0])
    y_count, xc_count = (column_ref.shape[0], out_ref.shape[0])
    side = pair_ref[0, 2 * tiles]
    for t in range(tiles):
        j = pair_ref[0, tiles + t]
        z, y = parted(j, y_count)
        from_column = column_ref[y, span(t if extra else z, vectors)]
        sums_ref[t] = lax.dot_general(
            from_column, tile_ref[t], (((1,), (1,)), ((), ())), preferred_element_type=F32
        )
    blank = jnp.zeros((2 * vectors, out_ref.shape[2]), BF16)
    for k in range(xc_count):
        out_ref[k, pl.ds(0, vectors)] = own_ref[...]
        out_ref[k, pl.ds(vectors, vectors)] = other_ref[...]
        out_ref[k, pl.ds(2 * vectors, 2 * vectors)] = blank
    if extra:
        total = jnp.zeros((ROWS, LANES), F32)
        for y in range(y_count):
            total += from_bits(column_ref[y, pl.ds(tiles * vectors, ROWS)])
        for k in range(xc_count):
            store_bits(out_ref, (k, pl.ds(4 * vectors, ROWS)), total)
    slots = []
    for t in range(tiles):
        i = pair_ref[0, t]
        half, xc = parted(i, xc_count)
        half = lax.bitwise_xor(half, side)
        slots.append((i, (xc, span(half, vectors, 2 * vectors))))
    store_sums(out_ref, slots, sums_ref)


def mirror_kernel(
    pair_ref, row_ref, tile_ref, near_ref, other_ref, out_ref, own_ref, far_ref, sums_ref
):
    tiles, vectors = (tile_ref.shape[0], own_ref.shape[0])
    y_count, xc_count = (out_ref.shape[0], row_ref.shape[0])
    extra = row_ref.shape[1] > 4 * vectors
    side = pair_ref[0, 2 * tiles]
    for t in range(tiles):
        half, xc = parted(pair_ref[0, t], xc_count)
        from_row = row_ref[xc, span(lax.bitwise_xor(half, side), vectors)]
        sums_ref[t] = jnp.dot(from_row, tile_ref[t], preferred_element_type=F32)
    sums = []
    for s in range(2):
        rows = pl.ds((2 + s) * vectors, vectors)
        total = row_ref[0, rows].astype(F32)
        for k in range(1, xc_count):
            total = total + row_ref[k, rows].astype(F32)
        sums.append(total)
    own_ref[...] = sums[0]
    far_ref[pl.ds(0, vectors)] = sums[1].astype(BF16)
    if extra:
        total = jnp.zeros((ROWS, LANES), F32)
        for k in range(xc_count):
            total += from_bits(row_ref[k, pl.ds(4 * vectors, ROWS)])
        store_bits(far_ref, (pl.ds(vectors, ROWS),), total)
        form = dot(near_ref[...].astype(F32), sums[0], 1, 1)
        form += dot(other_ref[...].astype(F32), sums[1], 1, 1)
        store_bits(far_ref, (pl.ds(vectors + ROWS, ROWS),), pack(form))
    for k in range(y_count):
        out_ref[k] = jnp.zeros(out_ref.shape[1:], BF16)
    if extra:
        for t in range(tiles):
            _, y = parted(pair_ref[0, tiles + t], y_count)
            out_ref[y, pl.ds(t * vectors, vectors)] = sums_ref[t].astype(BF16)
        return
    slots = []
    for t in range(tiles):
        j = pair_ref[0, tiles + t]
        z, y = parted(j, y_count)
        slots.append((j, (y, span(z, vectors))))
    store_sums(out_ref, slots, sums_ref)


def image_kernel(direct_ref, far_ref, mirror_ref, image_ref, current_ref, send_ref):
    image = direct_ref[...] + far_ref[...].astype(F32)
    for z in range(mirror_ref.shape[0]):
        image = image + mirror_ref[z].astype(F32)
    image_ref[...] = image
    current = image.astype(BF16)
    current_ref[...] = current
    gram = pack(dot(image, image, 1, 1))
    for z in range(send_ref.shape[0]):
        send_ref[z, pl.ds(0, image.shape[0])] = current
        store_bits(send_ref, (z, pl.ds(image.shape[0], ROWS)), gram)


def first_middle_kernel(mirror_ref, send_ref):
    vectors = send_ref.shape[1]
    for z in range(send_ref.shape[0]):
        rows = pl.ds(z * vectors, vectors)
        total = mirror_ref[0, rows].astype(F32)
        for y in range(1, mirror_ref.shape[0]):
            total = total + mirror_ref[y, rows].astype(F32)
        send_ref[z] = total.astype(BF16)


def second_middle_kernel(peer_ref, mirror_ref, sent_ref, far_ref, send_ref, sums_ref):
    y_count, vectors = (mirror_ref.shape[0], sums_ref.shape[1])
    sums_ref[...] = jnp.zeros_like(sums_ref)
    for y in range(y_count):
        for t in range(mirror_ref.shape[1] // vectors):
            z, _ = parted(peer_ref[y, t], y_count)
            sums_ref[z] = sums_ref[z] + mirror_ref[y, pl.ds(t * vectors, vectors)].astype(F32)
    rows = pl.ds(vectors + ROWS, ROWS)
    form = from_bits(sent_ref[rows]) + from_bits(far_ref[rows])
    for z in range(send_ref.shape[0]):
        send_ref[z, pl.ds(0, vectors)] = sums_ref[z].astype(BF16)
        store_bits(send_ref, (z, pl.ds(vectors, ROWS)), form)


def gram_kernel(sent_ref, far_ref, gram_ref, *, rows):
    place = pl.ds(gram_ref.shape[0], ROWS)
    both = from_bits(sent_ref[place]) + from_bits(far_ref[place])
    gram_ref[...] = unpack(both) * (1.0 / rows)


def last_kernel(direct_ref, far_ref, mirror_ref, image_ref, send_ref):
    vectors = image_ref.shape[0]
    form = jnp.zeros((ROWS, LANES), F32)
    for z in range(mirror_ref.shape[0]):
        form += from_bits(mirror_ref[z, pl.ds(vectors, ROWS)])
    for k in range(send_ref.shape[0]):
        store_bits(send_ref, (k, pl.ds(0, ROWS)), form)
    image = direct_ref[...] + far_ref[pl.ds(0, vectors)].astype(F32)
    for z in range(mirror_ref.shape[0]):
        image = image + mirror_ref[z, pl.ds(0, vectors)].astype(F32)
    image_ref[...] = image


def finish_kernel(bits_ref, inverse_ref, ritz_ref, last_ref, residual_ref, projected_ref, *, rows):
    form = jnp.zeros((ROWS, LANES), F32)
    for k in range(bits_ref.shape[0]):
        form += from_bits(bits_ref[k])
    form = unpack(form)
    inverse = inverse_ref[...]
    half = dot(inverse, (form + form.T) * (1.0 / rows), 1, 0)
    projected_ref[...] = dot(half, inverse, 1, 1)
    residual_ref[...] = last_ref[...] - dot(half, ritz_ref[...], 1, 0)


def product(pairs, tiles, current, send_z, note, peers):
    vectors, size = current.shape
    count = tiles.shape[0]
    y_count, z_count, xc_count = (lax.axis_size(Y), lax.axis_size(Z_LO), lax.axis_size(X_CORE))
    extra = send_z is not None
    if not extra:
        send_z = jnp.broadcast_to(current[None], (z_count, vectors, size))
    by_z = exchange(send_z, Z_LO)
    other = partner(current)
    if extra:
        select = functools.partial(select_kernel, vectors=vectors)
        out = ((y_count, count * vectors + ROWS, size), BF16)
        send = call(select, out)(peers, by_z)[0]
    else:
        out = ((y_count, z_count * vectors + ROWS, size), BF16)
        send = call(spread_kernel, out)(by_z, note)[0]
    column_block = exchange(send, Y)
    if not extra:
        peers = column_block[:, z_count * vectors, :LANES].astype(jnp.int32)
    send = call(
        functools.partial(direct_kernel, extra=extra),
        ((xc_count, 4 * vectors + ROWS * extra, size), BF16),
        scratch=[pltpu.VMEM((count, vectors, size), F32)],
    )(pairs, column_block, tiles, current, other)[0]
    arrived = exchange(send, X_CORE)
    send, own_direct, far = call(
        mirror_kernel,
        ((y_count, (count if extra else z_count) * vectors, size), BF16),
        ((vectors, size), F32),
        ((vectors + 2 * ROWS * extra, size), BF16),
        scratch=[pltpu.VMEM((count, vectors, size), F32)],
    )(pairs, arrived, tiles, current, other)
    mirror = exchange(send, Y)
    sent, far = (far, partner(far))
    out = ((z_count, vectors + ROWS * extra, size), BF16)
    if extra:
        scratch = [pltpu.VMEM((z_count, vectors, size), F32)]
        mirror = call(second_middle_kernel, out, scratch=scratch)(peers, mirror, sent, far)[0]
    else:
        mirror = call(first_middle_kernel, out)(mirror)[0]
    mirror = exchange(mirror, Z_LO)
    return own_direct, sent, far, mirror, peers


def steps(tile_values, tile_row, tile_col, basis_init):
    tiles = tile_values[0, 0]
    side = lax.axis_index(Z_HI).astype(jnp.int32)
    pairs = jnp.concatenate([tile_row[0], tile_col[0], side[None, None]], axis=1)
    pairs = jnp.pad(pairs, [(0, 0), (0, LANES - pairs.shape[1])])
    vectors, size = basis_init.shape
    total_rows = size * lax.axis_size(COL_ROW)

    note = jnp.pad(
        tile_col[0].astype(BF16), [(0, ROWS - 1), (0, size - tiles.shape[0])]
    )
    own_direct, _, far, mirror, peers = product(pairs, tiles, basis_init, None, note, None)
    image, current, send = call(
        image_kernel,
        ((vectors, size), F32),
        ((vectors, size), BF16),
        ((mirror.shape[0], vectors + ROWS, size), BF16),
    )(own_direct, far, mirror)
    own_direct, sent, far, mirror, _ = product(pairs, tiles, current, send, None, peers)
    raw_image, send = call(
        last_kernel,
        ((vectors, size), F32),
        ((lax.axis_size(Y_X_CORE), ROWS, 2 * LANES), BF16),
    )(own_direct, far, mirror)
    form = exchange(send, Y_X_CORE)
    gram = call(
        functools.partial(gram_kernel, rows=total_rows), ((vectors, vectors), F32)
    )(sent, far)[0]
    factor = jnp.linalg.cholesky(gram)
    inverse = lax.linalg.triangular_solve(
        factor, jnp.eye(vectors, dtype=F32), left_side=True, lower=True
    )
    ritz_basis = jnp.dot(inverse, image, precision=HIGHEST)
    last_image = jnp.dot(inverse, raw_image, precision=HIGHEST)
    turned = jnp.dot(inverse.T, ritz_basis, precision=HIGHEST)
    residual, projected = call(
        functools.partial(finish_kernel, rows=total_rows),
        ((vectors, size), F32),
        ((vectors, vectors), F32),
        out=jax.ShapeDtypeStruct,
    )(form, inverse, turned, last_image)
    return (ritz_basis, residual, projected)


def solution(mesh):
    finer = Mesh(mesh.devices.reshape(8, 4, 2, 4, 2), ("row_0", "row_1", "col_0", "col_1", "col_2"))
    placed = (P(ROW, COL, None, None, None), P(ROW, COL, None), P(ROW, COL, None), P(None, COL_ROW))
    return jax.shard_map(
        steps,
        mesh=finer,
        in_specs=placed,
        out_specs=(P(None, COL_ROW), P(None, COL_ROW), P()),
        check_vma=False,
    )
```

```python
import functools

import jax
import jax.numpy as jnp
from jax import lax
from jax.experimental import pallas as pl
from jax.experimental.pallas import tpu as pltpu
from jax.sharding import Mesh
from jax.sharding import PartitionSpec as P

Z_HI, X_CORE = ("col_0", ("col_1", "col_2"))
Z_LO, Y = ("row_0", "row_1")
Y_X_CORE = ("row_1", "col_1", "col_2")
COL = ("col_0", "col_1", "col_2")
ROW = ("row_0", "row_1")
COL_ROW = ("col_0", "col_1", "col_2", "row_0", "row_1")
HIGHEST = lax.Precision.HIGHEST
VMEM = pl.BlockSpec(memory_space=pltpu.VMEM)
F32, BF16 = (jnp.float32, jnp.bfloat16)


def placed(value):
    return pltpu.with_memory_space_constraint(value, pltpu.VMEM)


ROWS, LANES, VECTORS = (8, 128, 32)


def exchange(parts, axis):
    return lax.all_to_all(parts, axis, 0, 0, tiled=True)


def call(kernel, *outs, scratch=(), out=pltpu.VMEM):
    def run(*args):
        args = tuple(placed(arg) for arg in args)
        return pl.pallas_call(
            kernel,
            out_shape=tuple(out(shape, kind) for shape, kind in outs),
            in_specs=[VMEM] * len(args),
            out_specs=tuple(VMEM for _ in outs),
            scratch_shapes=list(scratch),
        )(*args)

    return run


def partner(value):
    return lax.ppermute(value, Z_HI, [(0, 1), (1, 0)])


def pack(small):
    return jnp.concatenate([small[k : k + ROWS] for k in range(0, small.shape[0], ROWS)], axis=1)


def unpack(packed):
    return jnp.concatenate([packed[:, k : k + VECTORS] for k in range(0, LANES, VECTORS)], axis=0)


def from_bits(bits):
    wide = bits.astype(F32)
    return wide[..., LANES:] + wide[..., :LANES]


def dot(left, right, left_dim, right_dim):
    return lax.dot_general(
        left, right, (((left_dim,), (right_dim,)), ((), ())),
        precision=HIGHEST, preferred_element_type=F32,
    )


def store_bits(out_ref, place, packed):
    high = packed.astype(BF16)
    out_ref[(*place, slice(0, LANES))] = high
    out_ref[(*place, slice(LANES, 2 * LANES))] = (packed - high.astype(F32)).astype(BF16)


def store_sums(out_ref, slots, sums_ref):
    for t, (index, place) in enumerate(slots):
        total = sums_ref[t]
        for other, (other_index, _) in enumerate(slots):
            if other != t:
                total = total + (other_index == index).astype(F32) * sums_ref[other]
        out_ref[place] = total.astype(BF16)


def parted(index, count):
    assert count & (count - 1) == 0
    return lax.shift_right_logical(index, count.bit_length() - 1), lax.bitwise_and(index, count - 1)


def span(slot, length, start=0):
    if isinstance(slot, int):
        return pl.ds(start + slot * length, length)
    return pl.ds(pl.multiple_of(start + slot * length, length), length)


def spread_kernel(by_z_ref, note_ref, out_ref):
    length = by_z_ref.shape[1]
    for y in range(out_ref.shape[0]):
        for z in range(by_z_ref.shape[0]):
            out_ref[y, pl.ds(z * length, length)] = by_z_ref[z]
        out_ref[y, pl.ds(by_z_ref.shape[0] * length, ROWS)] = note_ref[...]


def select_kernel(peer_ref, by_z_ref, out_ref, *, vectors):
    y_count = out_ref.shape[0]
    tiles = (out_ref.shape[1] - ROWS) // vectors
    total = jnp.zeros((ROWS, LANES), F32)
    for z in range(by_z_ref.shape[0]):
        total += from_bits(by_z_ref[z, pl.ds(vectors, ROWS)])
    for y in range(y_count):
        for t in range(tiles):
            place, _ = parted(peer_ref[y, t], y_count)
            out_ref[y, pl.ds(t * vectors, vectors)] = by_z_ref[place, pl.ds(0, vectors)]
        store_bits(out_ref, (y, pl.ds(tiles * vectors, ROWS)), total)


def direct_kernel(
    pair_ref, column_ref, tile_ref, own_ref, other_ref, out_ref, sums_ref, *, extra
):
    tiles, vectors = (tile_ref.shape[0], own_ref.shape[0])
    y_count, xc_count = (column_ref.shape[0], out_ref.shape[0])
    side = pair_ref[0, 2 * tiles]
    for t in range(tiles):
        j = pair_ref[0, tiles + t]
        z, y = parted(j, y_count)
        from_column = column_ref[y, span(t if extra else z, vectors)]
        sums_ref[t] = lax.dot_general(
            from_column, tile_ref[t], (((1,), (1,)), ((), ())), preferred_element_type=F32
        )
    blank = jnp.zeros((2 * vectors, out_ref.shape[2]), BF16)
    for k in range(xc_count):
        out_ref[k, pl.ds(0, vectors)] = own_ref[...]
        out_ref[k, pl.ds(vectors, vectors)] = other_ref[...]
        out_ref[k, pl.ds(2 * vectors, 2 * vectors)] = blank
    if extra:
        total = jnp.zeros((ROWS, LANES), F32)
        for y in range(y_count):
            total += from_bits(column_ref[y, pl.ds(tiles * vectors, ROWS)])
        for k in range(xc_count):
            store_bits(out_ref, (k, pl.ds(4 * vectors, ROWS)), total)
    slots = []
    for t in range(tiles):
        i = pair_ref[0, t]
        half, xc = parted(i, xc_count)
        half = lax.bitwise_xor(half, side)
        slots.append((i, (xc, span(half, vectors, 2 * vectors))))
    store_sums(out_ref, slots, sums_ref)


def mirror_kernel(
    pair_ref, row_ref, tile_ref, near_ref, other_ref, out_ref, own_ref, far_ref, sums_ref
):
    tiles, vectors = (tile_ref.shape[0], own_ref.shape[0])
    y_count, xc_count = (out_ref.shape[0], row_ref.shape[0])
    extra = row_ref.shape[1] > 4 * vectors
    side = pair_ref[0, 2 * tiles]
    for t in range(tiles):
        half, xc = parted(pair_ref[0, t], xc_count)
        from_row = row_ref[xc, span(lax.bitwise_xor(half, side), vectors)]
        sums_ref[t] = jnp.dot(from_row, tile_ref[t], preferred_element_type=F32)
    sums = []
    for s in range(2):
        rows = pl.ds((2 + s) * vectors, vectors)
        total = row_ref[0, rows].astype(F32)
        for k in range(1, xc_count):
            total = total + row_ref[k, rows].astype(F32)
        sums.append(total)
    own_ref[...] = sums[0]
    far_ref[pl.ds(0, vectors)] = sums[1].astype(BF16)
    if extra:
        total = jnp.zeros((ROWS, LANES), F32)
        for k in range(xc_count):
            total += from_bits(row_ref[k, pl.ds(4 * vectors, ROWS)])
        store_bits(far_ref, (pl.ds(vectors, ROWS),), total)
        form = dot(near_ref[...].astype(F32), sums[0], 1, 1)
        form += dot(other_ref[...].astype(F32), sums[1], 1, 1)
        store_bits(far_ref, (pl.ds(vectors + ROWS, ROWS),), pack(form))
    for k in range(y_count):
        out_ref[k] = jnp.zeros(out_ref.shape[1:], BF16)
    if extra:
        for t in range(tiles):
            _, y = parted(pair_ref[0, tiles + t], y_count)
            out_ref[y, pl.ds(t * vectors, vectors)] = sums_ref[t].astype(BF16)
        return
    slots = []
    for t in range(tiles):
        j = pair_ref[0, tiles + t]
        z, y = parted(j, y_count)
        slots.append((j, (y, span(z, vectors))))
    store_sums(out_ref, slots, sums_ref)


def image_kernel(direct_ref, far_ref, mirror_ref, image_ref, current_ref, send_ref):
    image = direct_ref[...] + far_ref[...].astype(F32)
    for z in range(mirror_ref.shape[0]):
        image = image + mirror_ref[z].astype(F32)
    image_ref[...] = image
    current = image.astype(BF16)
    current_ref[...] = current
    gram = pack(dot(image, image, 1, 1))
    for z in range(send_ref.shape[0]):
        send_ref[z, pl.ds(0, image.shape[0])] = current
        store_bits(send_ref, (z, pl.ds(image.shape[0], ROWS)), gram)


def first_middle_kernel(mirror_ref, send_ref):
    vectors = send_ref.shape[1]
    for z in range(send_ref.shape[0]):
        rows = pl.ds(z * vectors, vectors)
        total = mirror_ref[0, rows].astype(F32)
        for y in range(1, mirror_ref.shape[0]):
            total = total + mirror_ref[y, rows].astype(F32)
        send_ref[z] = total.astype(BF16)


def form_kernel(sent_ref, far_ref, send_ref, gram_ref, *, rows):
    vectors = gram_ref.shape[0]
    place = pl.ds(vectors, ROWS)
    gram_ref[...] = unpack(from_bits(sent_ref[place]) + from_bits(far_ref[place])) * (1.0 / rows)
    place = pl.ds(vectors + ROWS, ROWS)
    form = from_bits(sent_ref[place]) + from_bits(far_ref[place])
    for k in range(send_ref.shape[0]):
        store_bits(send_ref, (k, pl.ds(0, ROWS)), form)


def second_middle_kernel(peer_ref, mirror_ref, bits_ref, send_ref, sums_ref):
    y_count, vectors = (mirror_ref.shape[0], sums_ref.shape[1])
    sums_ref[...] = jnp.zeros_like(sums_ref)
    for y in range(y_count):
        for t in range(mirror_ref.shape[1] // vectors):
            z, _ = parted(peer_ref[y, t], y_count)
            sums_ref[z] = sums_ref[z] + mirror_ref[y, pl.ds(t * vectors, vectors)].astype(F32)
    form = jnp.zeros((ROWS, LANES), F32)
    for k in range(bits_ref.shape[0]):
        form += from_bits(bits_ref[k])
    for z in range(send_ref.shape[0]):
        send_ref[z, pl.ds(0, vectors)] = sums_ref[z].astype(BF16)
        store_bits(send_ref, (z, pl.ds(vectors, ROWS)), form)


def finish_kernel(
    mirror_ref, direct_ref, far_ref, inverse_ref, turned_ref, residual_ref, projected_ref, *, rows
):
    vectors = inverse_ref.shape[0]
    form = jnp.zeros((ROWS, LANES), F32)
    image = direct_ref[...] + far_ref[pl.ds(0, vectors)].astype(F32)
    for z in range(mirror_ref.shape[0]):
        form += from_bits(mirror_ref[z, pl.ds(vectors, ROWS)])
        image = image + mirror_ref[z, pl.ds(0, vectors)].astype(F32)
    form = unpack(form)
    inverse = inverse_ref[...]
    last_image = dot(inverse, image, 1, 0)
    half = dot(inverse, (form + form.T) * (1.0 / rows), 1, 0)
    projected_ref[...] = dot(half, inverse, 1, 1)
    residual_ref[...] = last_image - dot(half, turned_ref[...], 1, 0)


def product(pairs, tiles, current, send_z, note, peers):
    vectors, size = current.shape
    count = tiles.shape[0]
    y_count, z_count, xc_count = (lax.axis_size(Y), lax.axis_size(Z_LO), lax.axis_size(X_CORE))
    extra = send_z is not None
    if not extra:
        send_z = jnp.broadcast_to(current[None], (z_count, vectors, size))
    by_z = exchange(send_z, Z_LO)
    other = partner(current)
    if extra:
        select = functools.partial(select_kernel, vectors=vectors)
        out = ((y_count, count * vectors + ROWS, size), BF16)
        send = call(select, out)(peers, by_z)[0]
    else:
        out = ((y_count, z_count * vectors + ROWS, size), BF16)
        send = call(spread_kernel, out)(by_z, note)[0]
    column_block = exchange(send, Y)
    if not extra:
        peers = column_block[:, z_count * vectors, :LANES].astype(jnp.int32)
    send = call(
        functools.partial(direct_kernel, extra=extra),
        ((xc_count, 4 * vectors + ROWS * extra, size), BF16),
        scratch=[pltpu.VMEM((count, vectors, size), F32)],
    )(pairs, column_block, tiles, current, other)[0]
    arrived = exchange(send, X_CORE)
    send, own_direct, far = call(
        mirror_kernel,
        ((y_count, (count if extra else z_count) * vectors, size), BF16),
        ((vectors, size), F32),
        ((vectors + 2 * ROWS * extra, size), BF16),
        scratch=[pltpu.VMEM((count, vectors, size), F32)],
    )(pairs, arrived, tiles, current, other)
    mirror = exchange(send, Y)
    sent, far = (far, partner(far))
    if extra:
        form, gram = call(
            functools.partial(form_kernel, rows=size * lax.axis_size(COL_ROW)),
            ((lax.axis_size(Y_X_CORE), ROWS, 2 * LANES), BF16),
            ((vectors, vectors), F32),
        )(sent, far)
        form = exchange(form, Y_X_CORE)
        mirror = call(
            second_middle_kernel,
            ((z_count, vectors + ROWS, size), BF16),
            scratch=[pltpu.VMEM((z_count, vectors, size), F32)],
        )(peers, mirror, form)[0]
    else:
        mirror = call(first_middle_kernel, ((z_count, vectors, size), BF16))(mirror)[0]
        gram = None
    mirror = exchange(mirror, Z_LO)
    return own_direct, far, mirror, gram, peers


def steps(tile_values, tile_row, tile_col, basis_init):
    tiles = tile_values[0, 0]
    side = lax.axis_index(Z_HI).astype(jnp.int32)
    pairs = jnp.concatenate([tile_row[0], tile_col[0], side[None, None]], axis=1)
    pairs = jnp.pad(pairs, [(0, 0), (0, LANES - pairs.shape[1])])
    vectors, size = basis_init.shape
    total_rows = size * lax.axis_size(COL_ROW)

    note = jnp.pad(
        tile_col[0].astype(BF16), [(0, ROWS - 1), (0, size - tiles.shape[0])]
    )
    own_direct, far, mirror, _, peers = product(pairs, tiles, basis_init, None, note, None)
    image, current, send = call(
        image_kernel,
        ((vectors, size), F32),
        ((vectors, size), BF16),
        ((mirror.shape[0], vectors + ROWS, size), BF16),
    )(own_direct, far, mirror)
    own_direct, far, mirror, gram, _ = product(pairs, tiles, current, send, None, peers)
    factor = jnp.linalg.cholesky(gram)
    inverse = lax.linalg.triangular_solve(
        factor, jnp.eye(vectors, dtype=F32), left_side=True, lower=True
    )
    ritz_basis = jnp.dot(inverse, image, precision=HIGHEST)
    turned = jnp.dot(inverse.T, ritz_basis, precision=HIGHEST)
    residual, projected = call(
        functools.partial(finish_kernel, rows=total_rows),
        ((vectors, size), F32),
        ((vectors, vectors), F32),
        out=jax.ShapeDtypeStruct,
    )(mirror, own_direct, far, inverse, turned)
    return (ritz_basis, residual, projected)


def solution(mesh):
    finer = Mesh(mesh.devices.reshape(8, 4, 2, 4, 2), ("row_0", "row_1", "col_0", "col_1", "col_2"))
    placed = (P(ROW, COL, None, None, None), P(ROW, COL, None), P(ROW, COL, None), P(None, COL_ROW))
    return jax.shard_map(
        steps,
        mesh=finer,
        in_specs=placed,
        out_specs=(P(None, COL_ROW), P(None, COL_ROW), P()),
        check_vma=False,
    )
```

```python
import functools

import jax
import jax.numpy as jnp
from jax import lax
from jax.experimental import pallas as pl
from jax.experimental.pallas import tpu as pltpu
from jax.sharding import Mesh
from jax.sharding import PartitionSpec as P

Z_HI, X_CORE = ("col_0", ("col_1", "col_2"))
Z_LO, Y = ("row_0", "row_1")
Y_X_CORE = ("row_1", "col_1", "col_2")
COL = ("col_0", "col_1", "col_2")
ROW = ("row_0", "row_1")
COL_ROW = ("col_0", "col_1", "col_2", "row_0", "row_1")
HIGHEST = lax.Precision.HIGHEST
VMEM = pl.BlockSpec(memory_space=pltpu.VMEM)
F32, BF16 = (jnp.float32, jnp.bfloat16)


def placed(value):
    return pltpu.with_memory_space_constraint(value, pltpu.VMEM)


ROWS, LANES, VECTORS = (8, 128, 32)


def exchange(parts, axis):
    return lax.all_to_all(parts, axis, 0, 0, tiled=True)


def call(kernel, *outs, scratch=(), out=pltpu.VMEM):
    def run(*args):
        args = tuple(placed(arg) for arg in args)
        return pl.pallas_call(
            kernel,
            out_shape=tuple(out(shape, kind) for shape, kind in outs),
            in_specs=[VMEM] * len(args),
            out_specs=tuple(VMEM for _ in outs),
            scratch_shapes=list(scratch),
        )(*args)

    return run


def partner(value):
    return lax.ppermute(value, Z_HI, [(0, 1), (1, 0)])


def pack(small):
    return jnp.concatenate([small[k : k + ROWS] for k in range(0, small.shape[0], ROWS)], axis=1)


def unpack(packed):
    return jnp.concatenate([packed[:, k : k + VECTORS] for k in range(0, LANES, VECTORS)], axis=0)


def from_bits(bits):
    wide = bits.astype(F32)
    return wide[..., LANES:] + wide[..., :LANES]


def dot(left, right, left_dim, right_dim):
    return lax.dot_general(
        left, right, (((left_dim,), (right_dim,)), ((), ())),
        precision=HIGHEST, preferred_element_type=F32,
    )


def store_bits(out_ref, place, packed):
    high = packed.astype(BF16)
    out_ref[(*place, slice(0, LANES))] = high
    out_ref[(*place, slice(LANES, 2 * LANES))] = (packed - high.astype(F32)).astype(BF16)


def store_sums(out_ref, slots, sums_ref):
    for t, (index, place) in enumerate(slots):
        total = sums_ref[t]
        for other, (other_index, _) in enumerate(slots):
            if other != t:
                total = total + (other_index == index).astype(F32) * sums_ref[other]
        out_ref[place] = total.astype(BF16)


def parted(index, count):
    assert count & (count - 1) == 0
    return lax.shift_right_logical(index, count.bit_length() - 1), lax.bitwise_and(index, count - 1)


def span(slot, length, start=0):
    if isinstance(slot, int):
        return pl.ds(start + slot * length, length)
    return pl.ds(pl.multiple_of(start + slot * length, length), length)


def spread_kernel(by_z_ref, note_ref, out_ref):
    length = by_z_ref.shape[1]
    for y in range(out_ref.shape[0]):
        for z in range(by_z_ref.shape[0]):
            out_ref[y, pl.ds(z * length, length)] = by_z_ref[z]
        out_ref[y, pl.ds(by_z_ref.shape[0] * length, ROWS)] = note_ref[...]


def read_table(noted_ref, table_ref):
    for y in range(noted_ref.shape[0]):
        note = noted_ref[y, pl.ds(noted_ref.shape[1] - ROWS, ROWS), pl.ds(0, LANES)]
        table_ref[y] = note.astype(F32).astype(jnp.int32)


def select_kernel(noted_ref, by_z_ref, out_ref, table_ref, *, vectors):
    read_table(noted_ref, table_ref)
    y_count = out_ref.shape[0]
    tiles = (out_ref.shape[1] - ROWS) // vectors
    total = jnp.zeros((ROWS, LANES), F32)
    for z in range(by_z_ref.shape[0]):
        total += from_bits(by_z_ref[z, pl.ds(vectors, ROWS)])
    for y in range(y_count):
        for t in range(tiles):
            place, _ = parted(table_ref[y, 0, t], y_count)
            out_ref[y, pl.ds(t * vectors, vectors)] = by_z_ref[place, pl.ds(0, vectors)]
        store_bits(out_ref, (y, pl.ds(tiles * vectors, ROWS)), total)


def direct_kernel(
    pair_ref, column_ref, tile_ref, own_ref, other_ref, out_ref, sums_ref, *, extra
):
    tiles, vectors = (tile_ref.shape[0], own_ref.shape[0])
    y_count, xc_count = (column_ref.shape[0], out_ref.shape[0])
    side = pair_ref[0, 2 * tiles]
    for t in range(tiles):
        j = pair_ref[0, tiles + t]
        z, y = parted(j, y_count)
        from_column = column_ref[y, span(t if extra else z, vectors)]
        sums_ref[t] = lax.dot_general(
            from_column, tile_ref[t], (((1,), (1,)), ((), ())), preferred_element_type=F32
        )
    blank = jnp.zeros((2 * vectors, out_ref.shape[2]), BF16)
    for k in range(xc_count):
        out_ref[k, pl.ds(0, vectors)] = own_ref[...]
        out_ref[k, pl.ds(vectors, vectors)] = other_ref[...]
        out_ref[k, pl.ds(2 * vectors, 2 * vectors)] = blank
    if extra:
        total = jnp.zeros((ROWS, LANES), F32)
        for y in range(y_count):
            total += from_bits(column_ref[y, pl.ds(tiles * vectors, ROWS)])
        for k in range(xc_count):
            store_bits(out_ref, (k, pl.ds(4 * vectors, ROWS)), total)
    slots = []
    for t in range(tiles):
        i = pair_ref[0, t]
        half, xc = parted(i, xc_count)
        half = lax.bitwise_xor(half, side)
        slots.append((i, (xc, span(half, vectors, 2 * vectors))))
    store_sums(out_ref, slots, sums_ref)


def mirror_kernel(
    pair_ref, row_ref, tile_ref, near_ref, other_ref, out_ref, own_ref, far_ref, sums_ref
):
    tiles, vectors = (tile_ref.shape[0], own_ref.shape[0])
    y_count, xc_count = (out_ref.shape[0], row_ref.shape[0])
    extra = row_ref.shape[1] > 4 * vectors
    side = pair_ref[0, 2 * tiles]
    for t in range(tiles):
        half, xc = parted(pair_ref[0, t], xc_count)
        from_row = row_ref[xc, span(lax.bitwise_xor(half, side), vectors)]
        sums_ref[t] = jnp.dot(from_row, tile_ref[t], preferred_element_type=F32)
    sums = []
    for s in range(2):
        rows = pl.ds((2 + s) * vectors, vectors)
        total = row_ref[0, rows].astype(F32)
        for k in range(1, xc_count):
            total = total + row_ref[k, rows].astype(F32)
        sums.append(total)
    own_ref[...] = sums[0]
    far_ref[pl.ds(0, vectors)] = sums[1].astype(BF16)
    if extra:
        total = jnp.zeros((ROWS, LANES), F32)
        for k in range(xc_count):
            total += from_bits(row_ref[k, pl.ds(4 * vectors, ROWS)])
        store_bits(far_ref, (pl.ds(vectors, ROWS),), total)
        form = dot(near_ref[...].astype(F32), sums[0], 1, 1)
        form += dot(other_ref[...].astype(F32), sums[1], 1, 1)
        store_bits(far_ref, (pl.ds(vectors + ROWS, ROWS),), pack(form))
    for k in range(y_count):
        out_ref[k] = jnp.zeros(out_ref.shape[1:], BF16)
    for t in range(tiles):
        _, y = parted(pair_ref[0, tiles + t], y_count)
        out_ref[y, pl.ds(t * vectors, vectors)] = sums_ref[t].astype(BF16)


def image_kernel(direct_ref, far_ref, mirror_ref, image_ref, current_ref, send_ref):
    image = direct_ref[...] + far_ref[...].astype(F32)
    for z in range(mirror_ref.shape[0]):
        image = image + mirror_ref[z].astype(F32)
    image_ref[...] = image
    current = image.astype(BF16)
    current_ref[...] = current
    gram = pack(dot(image, image, 1, 1))
    for z in range(send_ref.shape[0]):
        send_ref[z, pl.ds(0, image.shape[0])] = current
        store_bits(send_ref, (z, pl.ds(image.shape[0], ROWS)), gram)


def sum_over_y(noted_ref, mirror_ref, sums_ref, table_ref):
    read_table(noted_ref, table_ref)
    y_count, vectors = (mirror_ref.shape[0], sums_ref.shape[1])
    sums_ref[...] = jnp.zeros_like(sums_ref)
    for y in range(y_count):
        for t in range(mirror_ref.shape[1] // vectors):
            z, _ = parted(table_ref[y, 0, t], y_count)
            sums_ref[z] = sums_ref[z] + mirror_ref[y, pl.ds(t * vectors, vectors)].astype(F32)


def first_middle_kernel(noted_ref, mirror_ref, send_ref, sums_ref, table_ref):
    sum_over_y(noted_ref, mirror_ref, sums_ref, table_ref)
    send_ref[...] = sums_ref[...].astype(BF16)


def form_kernel(sent_ref, far_ref, send_ref, gram_ref, *, rows):
    vectors = gram_ref.shape[0]
    place = pl.ds(vectors, ROWS)
    gram_ref[...] = unpack(from_bits(sent_ref[place]) + from_bits(far_ref[place])) * (1.0 / rows)
    place = pl.ds(vectors + ROWS, ROWS)
    form = from_bits(sent_ref[place]) + from_bits(far_ref[place])
    for k in range(send_ref.shape[0]):
        store_bits(send_ref, (k, pl.ds(0, ROWS)), form)


def second_middle_kernel(noted_ref, mirror_ref, bits_ref, send_ref, sums_ref, table_ref):
    sum_over_y(noted_ref, mirror_ref, sums_ref, table_ref)
    vectors = sums_ref.shape[1]
    form = jnp.zeros((ROWS, LANES), F32)
    for k in range(bits_ref.shape[0]):
        form += from_bits(bits_ref[k])
    for z in range(send_ref.shape[0]):
        send_ref[z, pl.ds(0, vectors)] = sums_ref[z].astype(BF16)
        store_bits(send_ref, (z, pl.ds(vectors, ROWS)), form)


def finish_kernel(
    mirror_ref, direct_ref, far_ref, inverse_ref, turned_ref, residual_ref, projected_ref, *, rows
):
    vectors = inverse_ref.shape[0]
    form = jnp.zeros((ROWS, LANES), F32)
    image = direct_ref[...] + far_ref[pl.ds(0, vectors)].astype(F32)
    for z in range(mirror_ref.shape[0]):
        form += from_bits(mirror_ref[z, pl.ds(vectors, ROWS)])
        image = image + mirror_ref[z, pl.ds(0, vectors)].astype(F32)
    form = unpack(form)
    inverse = inverse_ref[...]
    last_image = dot(inverse, image, 1, 0)
    half = dot(inverse, (form + form.T) * (1.0 / rows), 1, 0)
    projected_ref[...] = dot(half, inverse, 1, 1)
    residual_ref[...] = last_image - dot(half, turned_ref[...], 1, 0)


def product(pairs, tiles, current, send_z, note, noted):
    vectors, size = current.shape
    count = tiles.shape[0]
    y_count, z_count, xc_count = (lax.axis_size(Y), lax.axis_size(Z_LO), lax.axis_size(X_CORE))
    extra = send_z is not None
    table = pltpu.VMEM((y_count, ROWS, LANES), jnp.int32)
    if not extra:
        send_z = jnp.broadcast_to(current[None], (z_count, vectors, size))
    by_z = exchange(send_z, Z_LO)
    other = partner(current)
    if extra:
        select = functools.partial(select_kernel, vectors=vectors)
        out = ((y_count, count * vectors + ROWS, size), BF16)
        send = call(select, out, scratch=[table])(noted, by_z)[0]
    else:
        out = ((y_count, z_count * vectors + ROWS, size), BF16)
        send = call(spread_kernel, out)(by_z, note)[0]
    column_block = exchange(send, Y)
    if not extra:
        noted = column_block
    send = call(
        functools.partial(direct_kernel, extra=extra),
        ((xc_count, 4 * vectors + ROWS * extra, size), BF16),
        scratch=[pltpu.VMEM((count, vectors, size), F32)],
    )(pairs, column_block, tiles, current, other)[0]
    arrived = exchange(send, X_CORE)
    send, own_direct, far = call(
        mirror_kernel,
        ((y_count, count * vectors, size), BF16),
        ((vectors, size), F32),
        ((vectors + 2 * ROWS * extra, size), BF16),
        scratch=[pltpu.VMEM((count, vectors, size), F32)],
    )(pairs, arrived, tiles, current, other)
    mirror = exchange(send, Y)
    sent, far = (far, partner(far))
    sums = pltpu.VMEM((z_count, vectors, size), F32)
    if extra:
        form, gram = call(
            functools.partial(form_kernel, rows=size * lax.axis_size(COL_ROW)),
            ((lax.axis_size(Y_X_CORE), ROWS, 2 * LANES), BF16),
            ((vectors, vectors), F32),
        )(sent, far)
        form = exchange(form, Y_X_CORE)
        mirror = call(
            second_middle_kernel,
            ((z_count, vectors + ROWS, size), BF16),
            scratch=[sums, table],
        )(noted, mirror, form)[0]
    else:
        out = ((z_count, vectors, size), BF16)
        mirror = call(first_middle_kernel, out, scratch=[sums, table])(noted, mirror)[0]
        gram = None
    mirror = exchange(mirror, Z_LO)
    return own_direct, far, mirror, gram, noted


def steps(tile_values, tile_row, tile_col, basis_init):
    tiles = tile_values[0, 0]
    side = lax.axis_index(Z_HI).astype(jnp.int32)
    pairs = jnp.concatenate([tile_row[0], tile_col[0], side[None, None]], axis=1)
    pairs = jnp.pad(pairs, [(0, 0), (0, LANES - pairs.shape[1])])
    vectors, size = basis_init.shape
    total_rows = size * lax.axis_size(COL_ROW)

    note = jnp.pad(
        tile_col[0].astype(BF16), [(0, ROWS - 1), (0, size - tiles.shape[0])]
    )
    own_direct, far, mirror, _, noted = product(pairs, tiles, basis_init, None, note, None)
    image, current, send = call(
        image_kernel,
        ((vectors, size), F32),
        ((vectors, size), BF16),
        ((mirror.shape[0], vectors + ROWS, size), BF16),
    )(own_direct, far, mirror)
    own_direct, far, mirror, gram, _ = product(pairs, tiles, current, send, None, noted)
    factor = jnp.linalg.cholesky(gram)
    inverse = lax.linalg.triangular_solve(
        factor, jnp.eye(vectors, dtype=F32), left_side=True, lower=True
    )
    ritz_basis = jnp.dot(inverse, image, precision=HIGHEST)
    turned = jnp.dot(inverse.T, ritz_basis, precision=HIGHEST)
    residual, projected = call(
        functools.partial(finish_kernel, rows=total_rows),
        ((vectors, size), F32),
        ((vectors, vectors), F32),
        out=jax.ShapeDtypeStruct,
    )(mirror, own_direct, far, inverse, turned)
    return (ritz_basis, residual, projected)


def solution(mesh):
    finer = Mesh(mesh.devices.reshape(8, 4, 2, 4, 2), ("row_0", "row_1", "col_0", "col_1", "col_2"))
    placed = (P(ROW, COL, None, None, None), P(ROW, COL, None), P(ROW, COL, None), P(None, COL_ROW))
    return jax.shard_map(
        steps,
        mesh=finer,
        in_specs=placed,
        out_specs=(P(None, COL_ROW), P(None, COL_ROW), P()),
        check_vma=False,
    )
```

```python
import functools

import jax
import jax.numpy as jnp
from jax import lax
from jax.experimental import pallas as pl
from jax.experimental.pallas import tpu as pltpu
from jax.sharding import Mesh
from jax.sharding import PartitionSpec as P

Z_HI, X_CORE = ("col_0", ("col_1", "col_2"))
Z_LO, Y = ("row_0", "row_1")
Y_X_CORE = ("row_1", "col_1", "col_2")
COL = ("col_0", "col_1", "col_2")
ROW = ("row_0", "row_1")
COL_ROW = ("col_0", "col_1", "col_2", "row_0", "row_1")
HIGHEST = lax.Precision.HIGHEST
VMEM = pl.BlockSpec(memory_space=pltpu.VMEM)
F32, BF16 = (jnp.float32, jnp.bfloat16)


def placed(value):
    return pltpu.with_memory_space_constraint(value, pltpu.VMEM)


ROWS, LANES, VECTORS = (8, 128, 32)


def exchange(parts, axis):
    return lax.all_to_all(parts, axis, 0, 0, tiled=True)


def call(kernel, *outs, scratch=(), out=pltpu.VMEM):
    def run(*args):
        args = tuple(placed(arg) for arg in args)
        return pl.pallas_call(
            kernel,
            out_shape=tuple(out(shape, kind) for shape, kind in outs),
            in_specs=[VMEM] * len(args),
            out_specs=tuple(VMEM for _ in outs),
            scratch_shapes=list(scratch),
        )(*args)

    return run


def partner(value):
    return lax.ppermute(value, Z_HI, [(0, 1), (1, 0)])


def pack(small):
    return jnp.concatenate([small[k : k + ROWS] for k in range(0, small.shape[0], ROWS)], axis=1)


def unpack(packed):
    return jnp.concatenate([packed[:, k : k + VECTORS] for k in range(0, LANES, VECTORS)], axis=0)


def from_bits(bits):
    wide = bits.astype(F32)
    return wide[..., LANES:] + wide[..., :LANES]


def dot(left, right, left_dim, right_dim):
    return lax.dot_general(
        left, right, (((left_dim,), (right_dim,)), ((), ())),
        precision=HIGHEST, preferred_element_type=F32,
    )


def store_bits(out_ref, place, packed):
    high = packed.astype(BF16)
    out_ref[(*place, slice(0, LANES))] = high
    out_ref[(*place, slice(LANES, 2 * LANES))] = (packed - high.astype(F32)).astype(BF16)


def store_sums(out_ref, slots, sums_ref):
    for t, (index, place) in enumerate(slots):
        total = sums_ref[t]
        for other, (other_index, _) in enumerate(slots):
            if other != t:
                total = total + (other_index == index).astype(F32) * sums_ref[other]
        out_ref[place] = total.astype(BF16)


def parted(index, count):
    assert count & (count - 1) == 0
    return lax.shift_right_logical(index, count.bit_length() - 1), lax.bitwise_and(index, count - 1)


def span(slot, length, start=0):
    if isinstance(slot, int):
        return pl.ds(start + slot * length, length)
    return pl.ds(pl.multiple_of(start + slot * length, length), length)


def spread_kernel(by_z_ref, note_ref, out_ref):
    length = by_z_ref.shape[1]
    end = by_z_ref.shape[0] * length
    note = note_ref[...].astype(F32).astype(BF16)
    for y in range(out_ref.shape[0]):
        for z in range(by_z_ref.shape[0]):
            out_ref[y, pl.ds(z * length, length)] = by_z_ref[z]
        out_ref[y, pl.ds(end, ROWS)] = jnp.zeros((ROWS, out_ref.shape[2]), BF16)
        out_ref[y, pl.ds(end, 1), pl.ds(0, note.shape[1])] = note


def read_table(noted_ref, table_ref):
    for y in range(noted_ref.shape[0]):
        note = noted_ref[y, pl.ds(noted_ref.shape[1] - ROWS, ROWS), pl.ds(0, LANES)]
        table_ref[y] = note.astype(F32).astype(jnp.int32)


def select_kernel(noted_ref, by_z_ref, out_ref, table_ref, *, vectors):
    read_table(noted_ref, table_ref)
    y_count = out_ref.shape[0]
    tiles = (out_ref.shape[1] - ROWS) // vectors
    total = jnp.zeros((ROWS, LANES), F32)
    for z in range(by_z_ref.shape[0]):
        total += from_bits(by_z_ref[z, pl.ds(vectors, ROWS)])
    for y in range(y_count):
        for t in range(tiles):
            place, _ = parted(table_ref[y, 0, t], y_count)
            out_ref[y, pl.ds(t * vectors, vectors)] = by_z_ref[place, pl.ds(0, vectors)]
        store_bits(out_ref, (y, pl.ds(tiles * vectors, ROWS)), total)


def direct_kernel(
    pair_ref, column_ref, tile_ref, own_ref, other_ref, out_ref, sums_ref, *, extra
):
    tiles, vectors = (tile_ref.shape[0], own_ref.shape[0])
    y_count, xc_count = (column_ref.shape[0], out_ref.shape[0])
    side = pair_ref[0, 2 * tiles]
    for t in range(tiles):
        j = pair_ref[0, tiles + t]
        z, y = parted(j, y_count)
        from_column = column_ref[y, span(t if extra else z, vectors)]
        sums_ref[t] = lax.dot_general(
            from_column, tile_ref[t], (((1,), (1,)), ((), ())), preferred_element_type=F32
        )
    blank = jnp.zeros((2 * vectors, out_ref.shape[2]), BF16)
    for k in range(xc_count):
        out_ref[k, pl.ds(0, vectors)] = own_ref[...]
        out_ref[k, pl.ds(vectors, vectors)] = other_ref[...]
        out_ref[k, pl.ds(2 * vectors, 2 * vectors)] = blank
    if extra:
        total = jnp.zeros((ROWS, LANES), F32)
        for y in range(y_count):
            total += from_bits(column_ref[y, pl.ds(tiles * vectors, ROWS)])
        for k in range(xc_count):
            store_bits(out_ref, (k, pl.ds(4 * vectors, ROWS)), total)
    slots = []
    for t in range(tiles):
        i = pair_ref[0, t]
        half, xc = parted(i, xc_count)
        half = lax.bitwise_xor(half, side)
        slots.append((i, (xc, span(half, vectors, 2 * vectors))))
    store_sums(out_ref, slots, sums_ref)


def mirror_kernel(
    pair_ref, row_ref, tile_ref, near_ref, other_ref, out_ref, own_ref, far_ref, sums_ref
):
    tiles, vectors = (tile_ref.shape[0], own_ref.shape[0])
    y_count, xc_count = (out_ref.shape[0], row_ref.shape[0])
    extra = row_ref.shape[1] > 4 * vectors
    side = pair_ref[0, 2 * tiles]
    for t in range(tiles):
        half, xc = parted(pair_ref[0, t], xc_count)
        from_row = row_ref[xc, span(lax.bitwise_xor(half, side), vectors)]
        sums_ref[t] = jnp.dot(from_row, tile_ref[t], preferred_element_type=F32)
    sums = []
    for s in range(2):
        rows = pl.ds((2 + s) * vectors, vectors)
        total = row_ref[0, rows].astype(F32)
        for k in range(1, xc_count):
            total = total + row_ref[k, rows].astype(F32)
        sums.append(total)
    own_ref[...] = sums[0]
    far_ref[pl.ds(0, vectors)] = sums[1].astype(BF16)
    if extra:
        total = jnp.zeros((ROWS, LANES), F32)
        for k in range(xc_count):
            total += from_bits(row_ref[k, pl.ds(4 * vectors, ROWS)])
        store_bits(far_ref, (pl.ds(vectors, ROWS),), total)
        form = dot(near_ref[...].astype(F32), sums[0], 1, 1)
        form += dot(other_ref[...].astype(F32), sums[1], 1, 1)
        store_bits(far_ref, (pl.ds(vectors + ROWS, ROWS),), pack(form))
    for k in range(y_count):
        out_ref[k] = jnp.zeros(out_ref.shape[1:], BF16)
    for t in range(tiles):
        _, y = parted(pair_ref[0, tiles + t], y_count)
        out_ref[y, pl.ds(t * vectors, vectors)] = sums_ref[t].astype(BF16)


def image_kernel(direct_ref, far_ref, mirror_ref, image_ref, current_ref, send_ref):
    image = direct_ref[...] + far_ref[...].astype(F32)
    for z in range(mirror_ref.shape[0]):
        image = image + mirror_ref[z].astype(F32)
    image_ref[...] = image
    current = image.astype(BF16)
    current_ref[...] = current
    gram = pack(dot(image, image, 1, 1))
    for z in range(send_ref.shape[0]):
        send_ref[z, pl.ds(0, image.shape[0])] = current
        store_bits(send_ref, (z, pl.ds(image.shape[0], ROWS)), gram)


def sum_over_y(noted_ref, mirror_ref, sums_ref, table_ref):
    read_table(noted_ref, table_ref)
    y_count, vectors = (mirror_ref.shape[0], sums_ref.shape[1])
    sums_ref[...] = jnp.zeros_like(sums_ref)
    for y in range(y_count):
        for t in range(mirror_ref.shape[1] // vectors):
            z, _ = parted(table_ref[y, 0, t], y_count)
            sums_ref[z] = sums_ref[z] + mirror_ref[y, pl.ds(t * vectors, vectors)].astype(F32)


def first_middle_kernel(noted_ref, mirror_ref, send_ref, sums_ref, table_ref):
    sum_over_y(noted_ref, mirror_ref, sums_ref, table_ref)
    send_ref[...] = sums_ref[...].astype(BF16)


def form_kernel(sent_ref, far_ref, send_ref, gram_ref, *, rows):
    vectors = gram_ref.shape[0]
    place = pl.ds(vectors, ROWS)
    gram_ref[...] = unpack(from_bits(sent_ref[place]) + from_bits(far_ref[place])) * (1.0 / rows)
    place = pl.ds(vectors + ROWS, ROWS)
    form = from_bits(sent_ref[place]) + from_bits(far_ref[place])
    for k in range(send_ref.shape[0]):
        store_bits(send_ref, (k, pl.ds(0, ROWS)), form)


def second_middle_kernel(noted_ref, mirror_ref, bits_ref, send_ref, sums_ref, table_ref):
    sum_over_y(noted_ref, mirror_ref, sums_ref, table_ref)
    vectors = sums_ref.shape[1]
    form = jnp.zeros((ROWS, LANES), F32)
    for k in range(bits_ref.shape[0]):
        form += from_bits(bits_ref[k])
    for z in range(send_ref.shape[0]):
        send_ref[z, pl.ds(0, vectors)] = sums_ref[z].astype(BF16)
        store_bits(send_ref, (z, pl.ds(vectors, ROWS)), form)


def finish_kernel(
    mirror_ref, direct_ref, far_ref, inverse_ref, turned_ref, residual_ref, projected_ref, *, rows
):
    vectors = inverse_ref.shape[0]
    form = jnp.zeros((ROWS, LANES), F32)
    image = direct_ref[...] + far_ref[pl.ds(0, vectors)].astype(F32)
    for z in range(mirror_ref.shape[0]):
        form += from_bits(mirror_ref[z, pl.ds(vectors, ROWS)])
        image = image + mirror_ref[z, pl.ds(0, vectors)].astype(F32)
    form = unpack(form)
    inverse = inverse_ref[...]
    last_image = dot(inverse, image, 1, 0)
    half = dot(inverse, (form + form.T) * (1.0 / rows), 1, 0)
    projected_ref[...] = dot(half, inverse, 1, 1)
    residual_ref[...] = last_image - dot(half, turned_ref[...], 1, 0)


def product(pairs, tiles, current, send_z, note, noted):
    vectors, size = current.shape
    count = tiles.shape[0]
    y_count, z_count, xc_count = (lax.axis_size(Y), lax.axis_size(Z_LO), lax.axis_size(X_CORE))
    extra = send_z is not None
    table = pltpu.VMEM((y_count, ROWS, LANES), jnp.int32)
    if not extra:
        send_z = jnp.broadcast_to(current[None], (z_count, vectors, size))
    by_z = exchange(send_z, Z_LO)
    other = partner(current)
    if extra:
        select = functools.partial(select_kernel, vectors=vectors)
        out = ((y_count, count * vectors + ROWS, size), BF16)
        send = call(select, out, scratch=[table])(noted, by_z)[0]
    else:
        out = ((y_count, z_count * vectors + ROWS, size), BF16)
        send = call(spread_kernel, out)(by_z, note)[0]
    column_block = exchange(send, Y)
    if not extra:
        noted = column_block
    send = call(
        functools.partial(direct_kernel, extra=extra),
        ((xc_count, 4 * vectors + ROWS * extra, size), BF16),
        scratch=[pltpu.VMEM((count, vectors, size), F32)],
    )(pairs, column_block, tiles, current, other)[0]
    arrived = exchange(send, X_CORE)
    send, own_direct, far = call(
        mirror_kernel,
        ((y_count, count * vectors, size), BF16),
        ((vectors, size), F32),
        ((vectors + 2 * ROWS * extra, size), BF16),
        scratch=[pltpu.VMEM((count, vectors, size), F32)],
    )(pairs, arrived, tiles, current, other)
    mirror = exchange(send, Y)
    sent, far = (far, partner(far))
    sums = pltpu.VMEM((z_count, vectors, size), F32)
    if extra:
        form, gram = call(
            functools.partial(form_kernel, rows=size * lax.axis_size(COL_ROW)),
            ((lax.axis_size(Y_X_CORE), ROWS, 2 * LANES), BF16),
            ((vectors, vectors), F32),
        )(sent, far)
        form = exchange(form, Y_X_CORE)
        mirror = call(
            second_middle_kernel,
            ((z_count, vectors + ROWS, size), BF16),
            scratch=[sums, table],
        )(noted, mirror, form)[0]
    else:
        out = ((z_count, vectors, size), BF16)
        mirror = call(first_middle_kernel, out, scratch=[sums, table])(noted, mirror)[0]
        gram = None
    mirror = exchange(mirror, Z_LO)
    return own_direct, far, mirror, gram, noted


def steps(tile_values, tile_row, tile_col, basis_init):
    tiles = tile_values[0, 0]
    side = lax.axis_index(Z_HI).astype(jnp.int32)
    pairs = jnp.concatenate([tile_row[0], tile_col[0], side[None, None]], axis=1)
    pairs = jnp.pad(pairs, [(0, 0), (0, LANES - pairs.shape[1])])
    vectors, size = basis_init.shape
    total_rows = size * lax.axis_size(COL_ROW)

    own_direct, far, mirror, _, noted = product(pairs, tiles, basis_init, None, tile_col[0], None)
    image, current, send = call(
        image_kernel,
        ((vectors, size), F32),
        ((vectors, size), BF16),
        ((mirror.shape[0], vectors + ROWS, size), BF16),
    )(own_direct, far, mirror)
    own_direct, far, mirror, gram, _ = product(pairs, tiles, current, send, None, noted)
    factor = jnp.linalg.cholesky(gram)
    inverse = lax.linalg.triangular_solve(
        factor, jnp.eye(vectors, dtype=F32), left_side=True, lower=True
    )
    ritz_basis = jnp.dot(inverse, image, precision=HIGHEST)
    turned = jnp.dot(inverse.T, ritz_basis, precision=HIGHEST)
    residual, projected = call(
        functools.partial(finish_kernel, rows=total_rows),
        ((vectors, size), F32),
        ((vectors, vectors), F32),
        out=jax.ShapeDtypeStruct,
    )(mirror, own_direct, far, inverse, turned)
    return (ritz_basis, residual, projected)


def solution(mesh):
    finer = Mesh(mesh.devices.reshape(8, 4, 2, 4, 2), ("row_0", "row_1", "col_0", "col_1", "col_2"))
    placed = (P(ROW, COL, None, None, None), P(ROW, COL, None), P(ROW, COL, None), P(None, COL_ROW))
    return jax.shard_map(
        steps,
        mesh=finer,
        in_specs=placed,
        out_specs=(P(None, COL_ROW), P(None, COL_ROW), P()),
        check_vma=False,
    )
```

```python
import functools

import jax
import jax.numpy as jnp
from jax import lax
from jax.experimental import pallas as pl
from jax.experimental.pallas import tpu as pltpu
from jax.sharding import Mesh
from jax.sharding import PartitionSpec as P

Z_HI, X_CORE = ("col_0", ("col_1", "col_2"))
Z_LO, Y = ("row_0", "row_1")
Y_X_CORE = ("row_1", "col_1", "col_2")
COL = ("col_0", "col_1", "col_2")
ROW = ("row_0", "row_1")
COL_ROW = ("col_0", "col_1", "col_2", "row_0", "row_1")
HIGHEST = lax.Precision.HIGHEST
VMEM = pl.BlockSpec(memory_space=pltpu.VMEM)
F32, BF16 = (jnp.float32, jnp.bfloat16)


def placed(value):
    return pltpu.with_memory_space_constraint(value, pltpu.VMEM)


ROWS, LANES, VECTORS = (8, 128, 32)


def exchange(parts, axis):
    return lax.all_to_all(parts, axis, 0, 0, tiled=True)


def call(kernel, *outs, scratch=(), out=pltpu.VMEM):
    def run(*args):
        args = tuple(placed(arg) for arg in args)
        return pl.pallas_call(
            kernel,
            out_shape=tuple(out(shape, kind) for shape, kind in outs),
            in_specs=[VMEM] * len(args),
            out_specs=tuple(VMEM for _ in outs),
            scratch_shapes=list(scratch),
        )(*args)

    return run


def partner(value):
    return lax.ppermute(value, Z_HI, [(0, 1), (1, 0)])


def pack(small):
    return jnp.concatenate([small[k : k + ROWS] for k in range(0, small.shape[0], ROWS)], axis=1)


def unpack(packed):
    return jnp.concatenate([packed[:, k : k + VECTORS] for k in range(0, LANES, VECTORS)], axis=0)


def from_bits(bits):
    wide = bits.astype(F32)
    return wide[..., LANES:] + wide[..., :LANES]


def dot(left, right, left_dim, right_dim):
    return lax.dot_general(
        left, right, (((left_dim,), (right_dim,)), ((), ())),
        precision=HIGHEST, preferred_element_type=F32,
    )


def store_bits(out_ref, place, packed):
    high = packed.astype(BF16)
    out_ref[(*place, slice(0, LANES))] = high
    out_ref[(*place, slice(LANES, 2 * LANES))] = (packed - high.astype(F32)).astype(BF16)


def store_sums(out_ref, slots, sums_ref):
    for t, (index, place) in enumerate(slots):
        total = sums_ref[t]
        for other, (other_index, _) in enumerate(slots):
            if other != t:
                total = total + (other_index == index).astype(F32) * sums_ref[other]
        out_ref[place] = total.astype(BF16)


def parted(index, count):
    assert count & (count - 1) == 0
    return lax.shift_right_logical(index, count.bit_length() - 1), lax.bitwise_and(index, count - 1)


def span(slot, length, start=0):
    if isinstance(slot, int):
        return pl.ds(start + slot * length, length)
    return pl.ds(pl.multiple_of(start + slot * length, length), length)


def start_kernel(block_ref, send_ref, own_ref):
    own_ref[...] = block_ref[...]
    for z in range(send_ref.shape[0]):
        send_ref[z] = block_ref[...]


def spread_kernel(by_z_ref, note_ref, out_ref):
    length = by_z_ref.shape[1]
    end = by_z_ref.shape[0] * length
    note = note_ref[...].astype(F32).astype(BF16)
    for y in range(out_ref.shape[0]):
        for z in range(by_z_ref.shape[0]):
            out_ref[y, pl.ds(z * length, length)] = by_z_ref[z]
        out_ref[y, pl.ds(end, ROWS)] = jnp.zeros((ROWS, out_ref.shape[2]), BF16)
        out_ref[y, pl.ds(end, 1), pl.ds(0, note.shape[1])] = note


def read_table(noted_ref, table_ref):
    for y in range(noted_ref.shape[0]):
        note = noted_ref[y, pl.ds(noted_ref.shape[1] - ROWS, ROWS), pl.ds(0, LANES)]
        table_ref[y] = note.astype(F32).astype(jnp.int32)


def select_kernel(noted_ref, by_z_ref, out_ref, table_ref, *, vectors):
    read_table(noted_ref, table_ref)
    y_count = out_ref.shape[0]
    tiles = (out_ref.shape[1] - ROWS) // vectors
    total = jnp.zeros((ROWS, LANES), F32)
    for z in range(by_z_ref.shape[0]):
        total += from_bits(by_z_ref[z, pl.ds(vectors, ROWS)])
    for y in range(y_count):
        for t in range(tiles):
            place, _ = parted(table_ref[y, 0, t], y_count)
            out_ref[y, pl.ds(t * vectors, vectors)] = by_z_ref[place, pl.ds(0, vectors)]
        store_bits(out_ref, (y, pl.ds(tiles * vectors, ROWS)), total)


def direct_kernel(
    pair_ref, column_ref, tile_ref, own_ref, other_ref, out_ref, sums_ref, *, extra
):
    tiles, vectors = (tile_ref.shape[0], own_ref.shape[0])
    y_count, xc_count = (column_ref.shape[0], out_ref.shape[0])
    side = pair_ref[0, 2 * tiles]
    for t in range(tiles):
        j = pair_ref[0, tiles + t]
        z, y = parted(j, y_count)
        from_column = column_ref[y, span(t if extra else z, vectors)]
        sums_ref[t] = lax.dot_general(
            from_column, tile_ref[t], (((1,), (1,)), ((), ())), preferred_element_type=F32
        )
    blank = jnp.zeros((2 * vectors, out_ref.shape[2]), BF16)
    for k in range(xc_count):
        out_ref[k, pl.ds(0, vectors)] = own_ref[...]
        out_ref[k, pl.ds(vectors, vectors)] = other_ref[...]
        out_ref[k, pl.ds(2 * vectors, 2 * vectors)] = blank
    if extra:
        total = jnp.zeros((ROWS, LANES), F32)
        for y in range(y_count):
            total += from_bits(column_ref[y, pl.ds(tiles * vectors, ROWS)])
        for k in range(xc_count):
            store_bits(out_ref, (k, pl.ds(4 * vectors, ROWS)), total)
    slots = []
    for t in range(tiles):
        i = pair_ref[0, t]
        half, xc = parted(i, xc_count)
        half = lax.bitwise_xor(half, side)
        slots.append((i, (xc, span(half, vectors, 2 * vectors))))
    store_sums(out_ref, slots, sums_ref)


def mirror_kernel(
    pair_ref, row_ref, tile_ref, near_ref, other_ref, out_ref, own_ref, far_ref, sums_ref
):
    tiles, vectors = (tile_ref.shape[0], own_ref.shape[0])
    y_count, xc_count = (out_ref.shape[0], row_ref.shape[0])
    extra = row_ref.shape[1] > 4 * vectors
    side = pair_ref[0, 2 * tiles]
    for t in range(tiles):
        half, xc = parted(pair_ref[0, t], xc_count)
        from_row = row_ref[xc, span(lax.bitwise_xor(half, side), vectors)]
        sums_ref[t] = jnp.dot(from_row, tile_ref[t], preferred_element_type=F32)
    sums = []
    for s in range(2):
        rows = pl.ds((2 + s) * vectors, vectors)
        total = row_ref[0, rows].astype(F32)
        for k in range(1, xc_count):
            total = total + row_ref[k, rows].astype(F32)
        sums.append(total)
    own_ref[...] = sums[0]
    far_ref[pl.ds(0, vectors)] = sums[1].astype(BF16)
    if extra:
        total = jnp.zeros((ROWS, LANES), F32)
        for k in range(xc_count):
            total += from_bits(row_ref[k, pl.ds(4 * vectors, ROWS)])
        store_bits(far_ref, (pl.ds(vectors, ROWS),), total)
        form = dot(near_ref[...].astype(F32), sums[0], 1, 1)
        form += dot(other_ref[...].astype(F32), sums[1], 1, 1)
        store_bits(far_ref, (pl.ds(vectors + ROWS, ROWS),), pack(form))
    for k in range(y_count):
        out_ref[k] = jnp.zeros(out_ref.shape[1:], BF16)
    for t in range(tiles):
        _, y = parted(pair_ref[0, tiles + t], y_count)
        out_ref[y, pl.ds(t * vectors, vectors)] = sums_ref[t].astype(BF16)


def image_kernel(direct_ref, far_ref, mirror_ref, image_ref, current_ref, send_ref):
    image = direct_ref[...] + far_ref[...].astype(F32)
    for z in range(mirror_ref.shape[0]):
        image = image + mirror_ref[z].astype(F32)
    image_ref[...] = image
    current = image.astype(BF16)
    current_ref[...] = current
    gram = pack(dot(image, image, 1, 1))
    for z in range(send_ref.shape[0]):
        send_ref[z, pl.ds(0, image.shape[0])] = current
        store_bits(send_ref, (z, pl.ds(image.shape[0], ROWS)), gram)


def sum_over_y(noted_ref, mirror_ref, sums_ref, table_ref):
    read_table(noted_ref, table_ref)
    y_count, vectors = (mirror_ref.shape[0], sums_ref.shape[1])
    sums_ref[...] = jnp.zeros_like(sums_ref)
    for y in range(y_count):
        for t in range(mirror_ref.shape[1] // vectors):
            z, _ = parted(table_ref[y, 0, t], y_count)
            sums_ref[z] = sums_ref[z] + mirror_ref[y, pl.ds(t * vectors, vectors)].astype(F32)


def first_middle_kernel(noted_ref, mirror_ref, send_ref, sums_ref, table_ref):
    sum_over_y(noted_ref, mirror_ref, sums_ref, table_ref)
    send_ref[...] = sums_ref[...].astype(BF16)


def form_kernel(sent_ref, far_ref, send_ref, gram_ref, *, rows):
    vectors = gram_ref.shape[0]
    place = pl.ds(vectors, ROWS)
    gram_ref[...] = unpack(from_bits(sent_ref[place]) + from_bits(far_ref[place])) * (1.0 / rows)
    place = pl.ds(vectors + ROWS, ROWS)
    form = from_bits(sent_ref[place]) + from_bits(far_ref[place])
    for k in range(send_ref.shape[0]):
        store_bits(send_ref, (k, pl.ds(0, ROWS)), form)


def second_middle_kernel(noted_ref, mirror_ref, bits_ref, send_ref, sums_ref, table_ref):
    sum_over_y(noted_ref, mirror_ref, sums_ref, table_ref)
    vectors = sums_ref.shape[1]
    form = jnp.zeros((ROWS, LANES), F32)
    for k in range(bits_ref.shape[0]):
        form += from_bits(bits_ref[k])
    for z in range(send_ref.shape[0]):
        send_ref[z, pl.ds(0, vectors)] = sums_ref[z].astype(BF16)
        store_bits(send_ref, (z, pl.ds(vectors, ROWS)), form)


def finish_kernel(
    mirror_ref, direct_ref, far_ref, inverse_ref, turned_ref, residual_ref, projected_ref, *, rows
):
    vectors = inverse_ref.shape[0]
    form = jnp.zeros((ROWS, LANES), F32)
    image = direct_ref[...] + far_ref[pl.ds(0, vectors)].astype(F32)
    for z in range(mirror_ref.shape[0]):
        form += from_bits(mirror_ref[z, pl.ds(vectors, ROWS)])
        image = image + mirror_ref[z, pl.ds(0, vectors)].astype(F32)
    form = unpack(form)
    inverse = inverse_ref[...]
    last_image = dot(inverse, image, 1, 0)
    half = dot(inverse, (form + form.T) * (1.0 / rows), 1, 0)
    projected_ref[...] = dot(half, inverse, 1, 1)
    residual_ref[...] = last_image - dot(half, turned_ref[...], 1, 0)


def product(pairs, tiles, current, send_z, note, noted):
    vectors, size = current.shape
    count = tiles.shape[0]
    y_count, z_count, xc_count = (lax.axis_size(Y), lax.axis_size(Z_LO), lax.axis_size(X_CORE))
    extra = send_z is not None
    table = pltpu.VMEM((y_count, ROWS, LANES), jnp.int32)
    if not extra:
        send_z, current = pl.pallas_call(
            start_kernel,
            out_shape=(
                jax.ShapeDtypeStruct((z_count, vectors, size), BF16),
                pltpu.VMEM((vectors, size), BF16),
            ),
            in_specs=[VMEM],
            out_specs=(VMEM, VMEM),
        )(current)
    by_z = exchange(send_z, Z_LO)
    other = partner(current)
    if extra:
        select = functools.partial(select_kernel, vectors=vectors)
        out = ((y_count, count * vectors + ROWS, size), BF16)
        send = call(select, out, scratch=[table])(noted, by_z)[0]
    else:
        out = ((y_count, z_count * vectors + ROWS, size), BF16)
        send = call(spread_kernel, out)(by_z, note)[0]
    column_block = exchange(send, Y)
    if not extra:
        noted = column_block
    send = call(
        functools.partial(direct_kernel, extra=extra),
        ((xc_count, 4 * vectors + ROWS * extra, size), BF16),
        scratch=[pltpu.VMEM((count, vectors, size), F32)],
    )(pairs, column_block, tiles, current, other)[0]
    arrived = exchange(send, X_CORE)
    send, own_direct, far = call(
        mirror_kernel,
        ((y_count, count * vectors, size), BF16),
        ((vectors, size), F32),
        ((vectors + 2 * ROWS * extra, size), BF16),
        scratch=[pltpu.VMEM((count, vectors, size), F32)],
    )(pairs, arrived, tiles, current, other)
    mirror = exchange(send, Y)
    sent, far = (far, partner(far))
    sums = pltpu.VMEM((z_count, vectors, size), F32)
    if extra:
        form, gram = call(
            functools.partial(form_kernel, rows=size * lax.axis_size(COL_ROW)),
            ((lax.axis_size(Y_X_CORE), ROWS, 2 * LANES), BF16),
            ((vectors, vectors), F32),
        )(sent, far)
        form = exchange(form, Y_X_CORE)
        mirror = call(
            second_middle_kernel,
            ((z_count, vectors + ROWS, size), BF16),
            scratch=[sums, table],
        )(noted, mirror, form)[0]
    else:
        out = ((z_count, vectors, size), BF16)
        mirror = call(first_middle_kernel, out, scratch=[sums, table])(noted, mirror)[0]
        gram = None
    mirror = exchange(mirror, Z_LO)
    return own_direct, far, mirror, gram, noted


def steps(tile_values, tile_row, tile_col, basis_init):
    tiles = tile_values[0, 0]
    side = lax.axis_index(Z_HI).astype(jnp.int32)
    pairs = jnp.concatenate([tile_row[0], tile_col[0], side[None, None]], axis=1)
    pairs = jnp.pad(pairs, [(0, 0), (0, LANES - pairs.shape[1])])
    vectors, size = basis_init.shape
    total_rows = size * lax.axis_size(COL_ROW)

    own_direct, far, mirror, _, noted = product(pairs, tiles, basis_init, None, tile_col[0], None)
    image, current, send = call(
        image_kernel,
        ((vectors, size), F32),
        ((vectors, size), BF16),
        ((mirror.shape[0], vectors + ROWS, size), BF16),
    )(own_direct, far, mirror)
    own_direct, far, mirror, gram, _ = product(pairs, tiles, current, send, None, noted)
    factor = jnp.linalg.cholesky(gram)
    inverse = lax.linalg.triangular_solve(
        factor, jnp.eye(vectors, dtype=F32), left_side=True, lower=True
    )
    ritz_basis = jnp.dot(inverse, image, precision=HIGHEST)
    turned = jnp.dot(inverse.T, ritz_basis, precision=HIGHEST)
    residual, projected = call(
        functools.partial(finish_kernel, rows=total_rows),
        ((vectors, size), F32),
        ((vectors, vectors), F32),
        out=jax.ShapeDtypeStruct,
    )(mirror, own_direct, far, inverse, turned)
    return (ritz_basis, residual, projected)


def solution(mesh):
    finer = Mesh(mesh.devices.reshape(8, 4, 2, 4, 2), ("row_0", "row_1", "col_0", "col_1", "col_2"))
    placed = (P(ROW, COL, None, None, None), P(ROW, COL, None), P(ROW, COL, None), P(None, COL_ROW))
    return jax.shard_map(
        steps,
        mesh=finer,
        in_specs=placed,
        out_specs=(P(None, COL_ROW), P(None, COL_ROW), P()),
        check_vma=False,
    )
```
